32 devices in a mesh: grp: 4 (over y, x), pme: 8 (over z, core).
Axes of the slice: x: 2, y: 2, z: 4, core: 2. Of those that a mesh axis runs over, the one named last changes fastest.
Arguments:
- charge: float32 [4096], P(('grp', 'pme')), may hold values from -4 to 4
- base: int32 [3, 4096], P(None, ('grp', 'pme')), may hold values from 0 to 255, as said below
- frac: float32 [3, 4096], P(None, ('grp', 'pme')), may hold values from 0 to 1
- counts: int32 [32], P(('grp', 'pme')), may hold values from 16 to 128, as said below
- green: float32 [128, 256, 512], P('grp', 'pme'), may hold values from 0.05 to 0.5
Outputs:
- field: float32 [4, 4096], P(None, ('grp', 'pme'))
The draws below stay inside these ranges and needn't reach their ends.
Inputs may be any that keep to these rules, and one draw needn't show every extreme that they name: `base`: row 0 holds an atom's first mesh index along x (below 256), row 1 along y (below 256), row 2 the first of its four planes counted from the first plane of its slab (below 64). Block d's live atoms are its first counts[d] slots; other slots hold data that is ignored. Some block is full in every draw.
All inputs are finite; a program needn't handle non-finite values.
Results may differ from the reference program's by a relative error of at most 0.007.
Values may be sent and summed in bfloat16 or wider, within the bound.
A program may use at most 128 MiB of HBM per device.

```python
import math
import jax
import jax.numpy as jnp
from jax import lax

NX = 256
NY = 256
NZ = 512
A_DEV = 128
KX = 128
CZ = 64
BLOCKS = 32
ATOMS = 4096
N_PME = 8


def draw_base(key, part):
    keys = jax.random.split(jax.random.fold_in(key, 11), 3)
    along_x = jax.random.randint(keys[0], (ATOMS,), 0, NX)
    along_y = jax.random.randint(keys[1], (ATOMS,), 0, NY)
    along_z = jax.random.randint(keys[2], (ATOMS,), 0, CZ)
    return jnp.stack([along_x, along_y, along_z]).astype(jnp.int32)


def draw_counts(key, part):
    keys = jax.random.split(jax.random.fold_in(key, 23), 4)
    light = jax.random.randint(keys[0], (BLOCKS,), A_DEV // 8, A_DEV // 2 + 1)
    heavy = A_DEV - jax.random.randint(keys[1], (BLOCKS,), 0, A_DEV // 8 + 1)
    dense = jax.random.randint(keys[2], (BLOCKS,), 0, 4) == 0
    filled = jnp.where(dense, heavy, light)
    chosen = jax.random.randint(keys[3], (), 0, BLOCKS)
    filled = filled.at[chosen].set(A_DEV)
    return filled.astype(jnp.int32)


def steps_of(key, shape, shards, low, top_value):
    loudness = 1.0
    for axis_at, shards_of in shards:
        heights = jax.random.uniform(jax.random.fold_in(jax.random.fold_in(key, 6), axis_at), (shards_of,), jnp.float32, low / len(shards), top_value / len(shards))
        loudness = loudness * jnp.repeat(jnp.exp(heights), shape[axis_at] // shards_of).reshape((-1,) + (1,) * (len(shape) - 1 - axis_at))
    return loudness


def bell_draw(own_key, extent, width, limit, shards=(), held_as=jnp.bfloat16):
    array = jax.random.normal(own_key, extent, jnp.float32) * width
    if len(shards) > 0:
        array = steps_of(own_key, extent, shards, -0.22, 0.18) * array
    return jnp.clip(array, min=-limit, max=limit).astype(held_as)


def setup_inputs(seed: int = 0) -> dict:
    arg_keys = jax.random.split(jax.random.key(seed), 6)
    charge = bell_draw(arg_keys[0], (ATOMS,), 1.0, 4.0, ((0, 32),), jnp.float32)
    base = draw_base(jax.random.fold_in(arg_keys[5], 71), 0)
    frac = jnp.clip(1.0 * jax.random.uniform(arg_keys[2], (3, ATOMS), jnp.float32) ** steps_of(arg_keys[2], (3, ATOMS), ((1, 32),), -0.2, 0.2), 0.0, 1.0)
    counts = draw_counts(jax.random.fold_in(arg_keys[5], 71), 0)
    green = jnp.clip(jnp.exp(math.log(0.5) - 2.3025851 * jax.random.uniform(arg_keys[4], (KX, NY, NZ), jnp.float32) ** steps_of(arg_keys[4], (KX, NY, NZ), ((0, 4), (1, 8)), -0.2, 0.2)), 0.05, 0.5)
    return {"charge": charge, "base": base, "frac": frac, "counts": counts, "green": green}


TWO_PI = 2.0 * math.pi


def spline(coord):
    other = 1.0 - coord
    square = coord * coord
    cube = square * coord
    weights = jnp.stack([other * other * other / 6.0, (3.0 * cube - 6.0 * square + 4.0) / 6.0, (-3.0 * cube + 3.0 * square + 3.0 * coord + 1.0) / 6.0, cube / 6.0])
    slopes = jnp.stack([-other * other / 2.0, (3.0 * square - 4.0 * coord) / 2.0, (-3.0 * square + 2.0 * coord + 1.0) / 2.0, square / 2.0])
    return weights, slopes


def phase_parts(cell, first, count, modulus):
    waves = first + jnp.arange(count, dtype=jnp.int32)
    offsets = jnp.arange(4, dtype=jnp.int32)
    spots = (cell[None, :] + offsets[:, None]) % modulus
    turns = (spots[:, :, None] * waves[None, None, :]) % modulus
    angle = turns.astype(jnp.float32) * (TWO_PI / modulus)
    return jnp.cos(angle), jnp.sin(angle)


def combine(weights, cosine, sine):
    return jnp.sum(weights[:, :, None] * cosine, axis=0), -jnp.sum(weights[:, :, None] * sine, axis=0)


def to_bfloat(values):
    return lax.optimization_barrier(values.astype(jnp.bfloat16)).astype(jnp.float32)


def reference(charge, base, frac, counts, green):
    slots = jnp.arange(A_DEV, dtype=jnp.int32)
    live_all = (slots[None, :] < counts[:, None]).astype(jnp.float32)
    charges = charge.reshape(BLOCKS, A_DEV) * live_all
    cells = base.reshape(3, BLOCKS, A_DEV).transpose(1, 0, 2)
    coords = frac.reshape(3, BLOCKS, A_DEV).transpose(1, 0, 2)
    slab_index = (jnp.arange(BLOCKS, dtype=jnp.int32) % N_PME).astype(jnp.int32)
    offsets = jnp.arange(4, dtype=jnp.int32)

    def grid_rows(cell, slab):
        z_cells = (slab * CZ + cell[2][None, :] + offsets[:, None]) % NZ
        y_cells = (cell[1][None, :] + offsets[:, None]) % NY
        return (z_cells[:, None, :] * NY + y_cells[None, :, :]).reshape(-1)

    def deposit(grid, item):
        charge_here, cell, coord, slab = item
        x_weight, _ = spline(coord[0])
        y_weight, _ = spline(coord[1])
        z_weight, _ = spline(coord[2])
        cosine, sine = phase_parts(cell[0], 0, KX, NX)
        x_real, x_imag = combine(x_weight, cosine, sine)
        scaled = charge_here[None, :] * z_weight
        lead = jnp.stack([to_bfloat(scaled[:, :, None] * x_real[None]), to_bfloat(scaled[:, :, None] * x_imag[None])], axis=-1)
        y_low = to_bfloat(y_weight)
        update = lead[:, None] * y_low[None, :, :, None, None]
        grid = grid.at[grid_rows(cell, slab)].add(update.reshape(-1, KX, 2))
        return grid, None

    empty = jnp.zeros((NZ * NY, KX, 2), jnp.float32)
    grid, _ = lax.scan(deposit, empty, (charges, cells, coords, slab_index))
    grid = grid.reshape(NZ, NY, KX, 2)
    spectrum = (grid[..., 0] + 1j * grid[..., 1]).transpose(2, 1, 0)
    waves = jnp.fft.fftn(spectrum, axes=(1, 2))
    mesh_field = jnp.fft.ifftn(green * waves, axes=(1, 2))
    table = jnp.stack([to_bfloat(jnp.real(mesh_field)), to_bfloat(jnp.imag(mesh_field))], axis=-1)
    table = table.transpose(2, 1, 0, 3).reshape(NZ * NY, KX, 2)

    def sample(carry, item):
        charge_here, live, cell, coord, slab = item
        x_weight, x_slope = spline(coord[0])
        y_weight, y_slope = spline(coord[1])
        z_weight, z_slope = spline(coord[2])
        cosine, sine = phase_parts(cell[0], 0, KX, NX)
        x_real, x_imag = combine(x_weight, cosine, sine)
        slope_real, slope_imag = combine(x_slope, cosine, sine)
        values = table[grid_rows(cell, slab)].reshape(4, 4, A_DEV, KX, 2)
        plain_sum = jnp.sum(to_bfloat(y_weight)[None, :, :, None, None] * values, axis=1)
        slope_sum = jnp.sum(to_bfloat(y_slope)[None, :, :, None, None] * values, axis=1)
        level = jnp.sum(x_real[None] * plain_sum[..., 0] + x_imag[None] * plain_sum[..., 1], axis=-1)
        along_x = jnp.sum(slope_real[None] * plain_sum[..., 0] + slope_imag[None] * plain_sum[..., 1], axis=-1)
        along_y = jnp.sum(x_real[None] * slope_sum[..., 0] + x_imag[None] * slope_sum[..., 1], axis=-1)
        rows = jnp.stack([live * jnp.sum(z_weight * level, axis=0), charge_here * jnp.sum(z_weight * along_x, axis=0), charge_here * jnp.sum(z_weight * along_y, axis=0), charge_here * jnp.sum(z_slope * level, axis=0)])
        return carry, rows

    start = jnp.zeros((), jnp.float32)
    _, result = lax.scan(sample, start, (charges, live_all, cells, coords, slab_index))
    return result.transpose(1, 0, 2).reshape(4, BLOCKS * A_DEV)
```

```python
import functools
import math

import jax
import jax.numpy as jnp
import ml_dtypes
import numpy as np
from jax import lax
from jax.experimental import pallas as pl
from jax.experimental.pallas import tpu as pltpu
from jax.sharding import PartitionSpec as P

NX = 256
LANE = 128
REACH = 4
FINE = 8
PAD = 8
VMEM = pltpu.VMEM


def spline_weights(u):
    v = 1.0 - u
    u2 = u * u
    u3 = u2 * u
    return (
        v * v * v / 6.0,
        (3.0 * u3 - 6.0 * u2 + 4.0) / 6.0,
        (-3.0 * u3 + 3.0 * u2 + 3.0 * u + 1.0) / 6.0,
        u3 / 6.0,
    )


def spline_slopes(u):
    v = 1.0 - u
    u2 = u * u
    return (
        -v * v / 2.0,
        (3.0 * u2 - 4.0 * u) / 2.0,
        (-3.0 * u2 + 2.0 * u + 1.0) / 2.0,
        u2 / 2.0,
    )


def turn_parts(turns):
    x = (turns - jnp.floor(turns + 0.5)) * math.pi
    y = x * x
    s = 1.0 / 362880.0 - y * (1.0 / 39916800.0)
    s = -1.0 / 5040.0 + y * s
    s = 1.0 / 120.0 + y * s
    s = -1.0 / 6.0 + y * s
    s = x + x * (y * s)
    c = -1.0 / 3628800.0 + y * (1.0 / 479001600.0)
    c = 1.0 / 40320.0 + y * c
    c = -1.0 / 720.0 + y * c
    c = 1.0 / 24.0 + y * c
    c = -0.5 + y * c
    c = 1.0 + y * c
    return (1.0 - 2.0 * s * s, 2.0 * s * c)


def waves_of(weight_sets, cell, waves, steps):
    copies = cell.shape[1] // waves.shape[1]

    def widen(v):
        return jnp.concatenate([v] * copies, axis=1)

    cb, sb = turn_parts(widen(waves) * cell)
    cosines = [widen(c) for c, _ in steps]
    sines = [widen(s) for _, s in steps]
    out = []
    for w in weight_sets:
        gr = w[0] + sum(w[j + 1] * cosines[j] for j in range(REACH - 1))
        gi = sum(w[j + 1] * sines[j] for j in range(REACH - 1))
        out.append((cb * gr - sb * gi, -(cb * gi + sb * gr)))
    return out


def low(values):
    return values.astype(jnp.bfloat16).astype(jnp.float32)


def place(weights, cell, rows):
    z = lax.broadcasted_iota(jnp.int32, (rows, cell.shape[1]), 0) - cell
    total = jnp.where(z == 0, weights[0], 0.0)
    for j in range(1, REACH):
        total = jnp.where(z == j, weights[j], total)
    return total


def mesh_kernel(
    dims, counts_ref, charge_ref, frac_ref, base_ref, green_in, cos_in, sin_in, out_ref,
    mine_ref, atoms_ref, terms_ref, held_ref, green_ref, cos_ref, sin_ref,
    a_ref, b_ref, s_ref, h_ref, p_ref, x_ref, y_ref, sent, got, sent_terms, got_terms, staged
):
    kx, ky, nz, ny, planes, grp, per, chunks, slabs = dims
    group, slab = lax.axis_index("grp"), lax.axis_index("pme")
    me, total_slots, peer = ring_of(slabs, grp)
    wait = meet(total_slots, peer)
    stages = [
        pltpu.make_async_copy(source, target, staged.at[i])
        for i, (source, target) in enumerate(
            [(green_in, green_ref), (cos_in, cos_ref), (sin_in, sin_ref)]
        )
    ]
    for stage in stages:
        stage.start()
    live = live_of(counts_ref, charge_ref.shape)
    loaded = charge_ref[...] * live
    mine_ref[...] = jnp.concatenate(
        [loaded, frac_ref[...], base_ref[...].astype(jnp.float32), live], axis=0
    )
    own = pltpu.make_async_copy(mine_ref, atoms_ref.at[me], got.at[slab])
    own.start()
    count = kx * ky
    width = per * LANE
    tiles = nz // LANE
    fine = min(64, LANE)
    rows = fine + 16
    wide = ky % 16 == 0

    if wide:
        xk = lax.broadcasted_iota(jnp.int32, (kx, LANE), 0)
        yk = lax.broadcasted_iota(jnp.int32, (ky, LANE), 0)
    else:
        index = lax.broadcasted_iota(jnp.int32, (count, LANE), 0)
        xk, yk = index // ky, index % ky
    xk = (xk + group * kx).astype(jnp.float32) * (1.0 / NX)
    yk = (yk + slab * ky).astype(jnp.float32) * (1.0 / ny)
    x_steps = [turn_parts(xk * j) for j in range(1, REACH)]
    y_steps = [turn_parts(yk * j) for j in range(1, REACH)]

    s_ref[...] = jnp.zeros_like(s_ref)
    dot = functools.partial(jnp.dot, preferred_element_type=jnp.float32)
    half = nz // 2
    scale = 1.0 / (ny * nz)
    for stage in stages:
        stage.wait()
    lane_in = lax.broadcasted_iota(jnp.int32, (nz, nz), 0)
    lane_out = lax.broadcasted_iota(jnp.int32, (nz, nz), 1)
    wanted = jnp.where(lane_out < half, 2 * lane_out, 2 * (lane_out - half) + 1)
    order = jnp.where(lane_in == wanted, 1.0, 0.0).astype(jnp.bfloat16)
    block = min(256, count)
    for k in range(0, count, block):
        whole = green_ref[k : k + block] * scale
        high = whole.astype(jnp.bfloat16)
        rest = (whole - high.astype(jnp.float32)).astype(jnp.bfloat16)
        green_ref[k : k + block] = dot(high, order) + dot(rest, order)
    wait()

    def send(i, carry):
        pltpu.make_async_remote_copy(
            src_ref=mine_ref,
            dst_ref=atoms_ref.at[me],
            send_sem=sent,
            recv_sem=got.at[slab],
            **peer(i)[1],
        ).start()
        return carry

    lax.fori_loop(1, total_slots, send, 0)
    share = grp // per

    def turn_to(i, ahead):
        return (slab + ahead + i // share) % slabs * share + i % share

    def load(c):
        return jnp.concatenate([atoms_ref[c * per + i] for i in range(per)], axis=1)

    def tables(rec):
        fx, fy = rec[1:2], rec[2:3]
        wx = [spline_weights(fx), spline_slopes(fx)]
        wy = [[low(w) for w in spline_weights(fy)], [low(w) for w in spline_slopes(fy)]]
        return waves_of(wx, rec[4:5], xk, x_steps), waves_of(wy, rec[5:6], yk, y_steps)

    def keep(c, rec):
        for kind, (x, y) in enumerate(zip(*tables(rec))):
            for part in range(2):
                x_ref[c, 2 * kind + part] = x[part]
                y_ref[c, 2 * kind + part] = y[part].astype(jnp.bfloat16)

    def row_of(c, kind, i):
        return [
            jnp.broadcast_to(x_ref[c, 2 * kind + part, i : i + 1], (16, width)).astype(jnp.bfloat16)
            for part in range(2)
        ]

    def product(ref, lead, c, x_kind, y_kind, made):
        if not wide:
            (xr, xi), (yr, yi) = made[0][x_kind], made[1][y_kind]
            ref[lead + (slice(0, count),)] = (xr * yr - xi * yi).astype(jnp.bfloat16)
            ref[lead + (slice(count, 2 * count),)] = (xr * yi + xi * yr).astype(jnp.bfloat16)
            return
        for i in range(kx):
            row = row_of(c, x_kind, i)
            for j in range(0, ky, 16):
                yr = y_ref[c, 2 * y_kind, j : j + 16]
                yi = y_ref[c, 2 * y_kind + 1, j : j + 16]
                at = i * ky + j
                ref[lead + (slice(at, at + 16),)] = row[0] * yr - row[1] * yi
                ref[lead + (slice(count + at, count + at + 16),)] = row[0] * yi + row[1] * yr

    def arrive(i):
        c = turn_to(i, 0)

        @pl.when(i % share == 0)
        def _():
            part = atoms_ref.at[pl.ds(c * per, grp)]
            pltpu.make_async_copy(part, part, got.at[c // share]).wait()

        return c

    def spread(i, carry):
        c = arrive(i)
        rec = load(c)
        start = (c * per) // grp * planes
        tile = start // LANE
        cell = rec[6:7].astype(jnp.int32) + (start - tile * LANE)
        wz = [rec[0:1] * w for w in spline_weights(rec[3:4])]
        table = place(wz, cell, LANE + 16).astype(jnp.bfloat16)
        rest = jnp.zeros((LANE - 16, width), jnp.bfloat16)
        table = jnp.concatenate([table, rest], axis=0)
        following = lax.rem(tile + 1, tiles)

        def add(at, size, block):
            part = lax.dot_general(
                block, table, (((1,), (1,)), ((), ())), preferred_element_type=jnp.float32
            )
            s_ref[tile, at : at + size] += part[:, :LANE]
            s_ref[following, at : at + size] += part[:, LANE:]

        if not wide:
            product(a_ref, (c,), c, 0, 0, tables(rec))
            add(0, 2 * count, a_ref[c])
            return carry
        keep(c, rec)
        some = max(1, 256 // ky)
        for i0 in range(0, kx, some):
            blocks = ([], [])
            for k in range(i0, min(i0 + some, kx)):
                row = row_of(c, 0, k)
                for j in range(0, ky, 16):
                    yr, yi = y_ref[c, 0, j : j + 16], y_ref[c, 1, j : j + 16]
                    blocks[0].append(row[0] * yr - row[1] * yi)
                    blocks[1].append(row[0] * yi + row[1] * yr)
            for part in range(2):
                block = jnp.concatenate(blocks[part], axis=0)
                at, size = part * count + i0 * ky, block.shape[0]
                a_ref[c, at : at + size] = block
                add(at, size, block)
        return carry

    lax.fori_loop(0, chunks, spread, 0)

    def dot_t(a, b):
        return lax.dot_general(a, b, (((1,), (1,)), ((), ())), preferred_element_type=jnp.float32)

    def near(values):
        return values.astype(jnp.bfloat16)

    middle = tiles // 2
    for k in range(0, count, block):
        back = []
        parts = []
        for at in (k, count + k):
            first = jnp.concatenate([s_ref[t, at : at + block] for t in range(middle)], axis=1)
            last = jnp.concatenate([s_ref[t, at : at + block] for t in range(middle, tiles)], axis=1)
            parts.append((near(first + last), near(first - last)))
        for odd in range(2):
            cosine, sine = cos_ref[odd], sin_ref[odd]
            sr, si = parts[0][odd], parts[1][odd]
            factor = green_ref[k : k + block, odd * half : (odd + 1) * half]
            hr = near((dot(sr, cosine) + dot(si, sine)) * factor)
            hi = near((dot(si, cosine) - dot(sr, sine)) * factor)
            back.append((dot_t(cosine, hr) - dot_t(sine, hi), dot_t(cosine, hi) + dot_t(sine, hr)))
        for part, at in enumerate((k, count + k)):
            even, odd = back[0][part], back[1][part]
            lower = near(even + odd)
            p_ref[0:half, at : at + block] = lower
            p_ref[half:nz, at : at + block] = near(even - odd)
            p_ref[nz : nz + 16, at : at + block] = lower[0:16]

    def gather(i, carry):
        c = turn_to(i, 1)
        rec = load(c)
        made = None if wide else tables(rec)
        product(b_ref, (), c, 1, 0, made)
        product(h_ref, (), c, 0, 1, made)
        start = (c * per) // grp * planes
        base = start // fine * fine
        cell = rec[6:7].astype(jnp.int32) + (start - base)
        window = p_ref[pl.ds(pl.multiple_of(base, 16), rows), :]
        level = dot(window, a_ref[c])
        along_x = dot(window, b_ref[...])
        along_y = dot(window, h_ref[...])
        wz = place(spline_weights(rec[3:4]), cell, rows)
        dz = place(spline_slopes(rec[3:4]), cell, rows)

        def total(values):
            return jnp.sum(values, axis=0, keepdims=True)

        terms = jnp.concatenate(
            [total(wz * level), total(wz * along_x), total(wz * along_y), total(dz * level)], axis=0
        )
        for j in range(per):
            at = c * per + j
            terms_ref[at] = terms[:, j * LANE : (j + 1) * LANE]

            @pl.when(at == me)
            def _():
                pltpu.make_async_copy(terms_ref.at[at], held_ref.at[me], got_terms).start()

            @pl.when(at != me)
            def _():
                pltpu.make_async_remote_copy(
                    src_ref=terms_ref.at[at],
                    dst_ref=held_ref.at[me],
                    send_sem=sent_terms,
                    recv_sem=got_terms,
                    device_id=(at % grp, at // grp),
                    device_id_type=pl.DeviceIdType.MESH,
                ).start()

        return carry

    lax.fori_loop(0, chunks, gather, 0)
    all_sent(held_ref, total_slots, got_terms)
    all_sent(held_ref, total_slots - 1, sent_terms)
    all_sent(atoms_ref, total_slots - 1, sent)
    factors = jnp.concatenate([live, loaded, loaded, loaded], axis=0)
    out_ref[...] = jnp.sum(held_ref[...], axis=0) * factors

def digits(value, radix):
    return value // radix, value % radix


def slab_kernel(
    dims, counts_ref, charge_ref, frac_ref, base_ref, green_in, ahead_in, back_in, out_ref,
    mine_ref, atoms_ref, terms_ref, held_ref, green_ref, turned_ref, ahead_ref, back_ref,
    s_ref, p_ref, x_ref, y_ref, spots_ref, z_ref, sent, got, sent_terms, got_terms, staged
):
    kx, ky, nz, ny, planes, grp, slabs, fine = dims
    group, slab = lax.axis_index("grp"), lax.axis_index("pme")
    me, total_slots, peer = ring_of(slabs, grp)
    wait = meet(total_slots, peer)
    stages = [
        pltpu.make_async_copy(source, target, staged.at[i])
        for i, (source, target) in enumerate(
            [(green_in, green_ref), (ahead_in, ahead_ref), (back_in, back_ref)]
        )
    ]
    for stage in stages:
        stage.start()
    live = live_of(counts_ref, charge_ref.shape)
    loaded = charge_ref[...] * live
    mine_ref[...] = jnp.concatenate(
        [loaded, frac_ref[...], base_ref[...].astype(jnp.float32), live], axis=0
    )
    own = pltpu.make_async_copy(mine_ref, atoms_ref.at[me], got.at[slab])
    own.start()

    atoms = charge_ref.shape[1]
    width = grp * atoms
    groups = LANE // ky
    spots = planes // fine
    tiles = spots // groups
    lanes = spots * ky
    reach = fine + REACH - 1
    tall = slabs * fine
    pitch = tall + PAD
    drift = kx + PAD
    quarter = nz // 4
    low_type = jnp.bfloat16
    f32 = jnp.float32
    dot = functools.partial(jnp.dot, preferred_element_type=f32)

    def dot_t(a, b):
        return lax.dot_general(a, b, (((1,), (1,)), ((), ())), preferred_element_type=f32)

    xk = (lax.broadcasted_iota(jnp.int32, (kx, LANE), 0) + group * kx).astype(f32) * (1.0 / NX)
    yk = (lax.broadcasted_iota(jnp.int32, (ky, LANE), 0) + slab * ky).astype(f32) * (1.0 / ny)
    x_steps = [turn_parts(xk * j) for j in range(1, REACH)]
    y_steps = [turn_parts(yk * j) for j in range(1, REACH)]

    for part in range(2):
        for t in range(tiles):
            for z in range(REACH - 1):
                for p in range(slabs):
                    s_ref[part, t, pl.ds(p * fine + z, kx, stride=pitch), :] = jnp.zeros((kx, LANE), f32)
    for stage in stages:
        stage.wait()
    row = lax.broadcasted_iota(jnp.int32, (nz, nz), 0)
    column = lax.broadcasted_iota(jnp.int32, (nz, nz), 1)
    wanted = 4 * (row % quarter) + row // quarter
    order = jnp.where(column == wanted, 1.0, 0.0).astype(low_type)
    scale = 1.0 / (ny * nz)
    block = 2 * LANE
    for k in range(0, kx * ky, block):
        whole = green_ref[k : k + block] * scale
        high = whole.astype(low_type)
        rest = (whole - high.astype(f32)).astype(low_type)
        turned_ref[:, k : k + block] = dot_t(order, high) + dot_t(order, rest)
    wait()

    def send(i, carry):
        pltpu.make_async_remote_copy(
            src_ref=mine_ref,
            dst_ref=atoms_ref.at[me],
            send_sem=sent,
            recv_sem=got.at[slab],
            **peer(i)[1],
        ).start()
        return carry

    lax.fori_loop(1, total_slots, send, 0)

    def load(c):
        return jnp.concatenate([atoms_ref[c * grp + i] for i in range(grp)], axis=1)

    def cells(rec):
        cell = rec[6:7].astype(jnp.int32)
        return digits(cell, fine)

    def spread(i, carry):
        c = (slab + i) % slabs
        part = atoms_ref.at[pl.ds(c * grp, grp)]
        pltpu.make_async_copy(part, part, got.at[c]).wait()
        rec = load(c)
        fx, fy, fz = rec[1:2], rec[2:3], rec[3:4]
        wx = [spline_weights(fx), spline_slopes(fx)]
        wy = [[low(w) for w in spline_weights(fy)], [low(w) for w in spline_slopes(fy)]]
        xs = waves_of(wx, rec[4:5], xk, x_steps)
        ys = waves_of(wy, rec[5:6], yk, y_steps)
        for kind in range(2):
            for part in range(2):
                x_ref[c, 2 * kind + part] = xs[kind][part]
        for part in range(2):
            y_ref[c, part] = ys[1][part].astype(low_type)
        spot, cell = cells(rec)
        y_low = [ys[0][part].astype(low_type) for part in range(2)]
        for z in range(spots):
            here = jnp.broadcast_to(jnp.where(spot == z, 1.0, 0.0), (ky, width)).astype(low_type)
            for part in range(2):
                at = part * lanes + z * ky
                spots_ref[c, at : at + ky] = y_low[part] * here
        wz = place(spline_weights(fz), cell, 16)
        z_ref[0] = wz
        x_low = [(xs[0][part] * rec[0:1]).astype(low_type) for part in range(2)]
        rows = []
        for z in range(reach):
            weight = jnp.broadcast_to(z_ref[0, z : z + 1], (kx, width)).astype(low_type)
            rows += [x_low[0] * weight, x_low[1] * weight]
        made = dot_t(jnp.concatenate(rows, axis=0), spots_ref[c])

        def mesh_rows(z):
            at = 2 * z * kx
            real, imag = made[at : at + kx], made[at + kx : at + 2 * kx]
            return (
                real[:, :lanes] - imag[:, lanes:],
                real[:, lanes:] + imag[:, :lanes],
            )

        following = (c + 1) % slabs
        first = lax.broadcasted_iota(jnp.int32, (kx, lanes), 1) < ky
        for z in range(fine):
            values = mesh_rows(z)
            past = mesh_rows(z + fine) if z + fine < reach else None
            for part in range(2):
                value = values[part]
                if past is not None:
                    moved = jnp.concatenate(
                        [past[part][:, lanes - ky :], past[part][:, : lanes - ky]], axis=1
                    )
                    value = value + jnp.where(first, 0.0, moved)
                for t in range(tiles):
                    at = pl.ds(c * fine + z, kx, stride=pitch)
                    out = value[:, t * LANE : (t + 1) * LANE]
                    if past is not None:
                        out = out + s_ref[part, t, at, :]
                    s_ref[part, t, at, :] = out
                if past is not None:
                    at = pl.ds(following * fine + z, kx, stride=pitch)
                    s_ref[part, 0, at, :] += jnp.where(first, moved, 0.0)[:, :LANE]
        return carry

    lax.fori_loop(0, slabs, spread, 0)

    side = groups * LANE
    row = lax.broadcasted_iota(jnp.int32, (side, side), 0)
    column = lax.broadcasted_iota(jnp.int32, (side, side), 1)
    wanted = (row % LANE) // ky * LANE + row // LANE * ky + row % ky
    swap = jnp.where(column == wanted, 1.0, 0.0).astype(low_type)
    fewer = slabs // 4
    piece = fewer * fine
    pair = 2

    def near(values):
        return values.astype(low_type)

    def transform(step, carry):
        picked = []
        for part in range(2):
            halves = []
            for h in range(pair):
                k0 = (step * pair + h) * groups
                left = jnp.concatenate(
                    [
                        jnp.concatenate(
                            [
                                s_ref[part, t, pl.ds(pl.multiple_of((k0 + u) * pitch, 8), tall), :]
                                for u in range(groups)
                            ],
                            axis=1,
                        )
                        for t in range(tiles)
                    ],
                    axis=0,
                )
                halves.append(dot(near(left), swap))
            quarters = []
            for m in range(4):
                blocks = []
                for g in range(groups):
                    for t in range(tiles):
                        at = t * tall + m * piece
                        blocks.append(
                            jnp.concatenate(
                                [half[at : at + piece, g * LANE : (g + 1) * LANE] for half in halves], axis=1
                            )
                        )
                quarters.append(jnp.concatenate(blocks, axis=0))
            picked.append(quarters)
        re, im = picked
        ar, ai, br, bi = re[0] + re[2], im[0] + im[2], re[0] - re[2], im[0] - im[2]
        cr, ci, dr, di = re[1] + re[3], im[1] + im[3], re[1] - re[3], im[1] - im[3]
        mixed = [(ar + cr, ai + ci), (br + di, bi - dr), (ar - cr, ai - ci), (br - di, bi + dr)]
        back = []
        for r in range(4):
            stacked = jnp.concatenate([near(mixed[r][0]), near(mixed[r][1])], axis=0)
            waves = dot(ahead_ref[r], stacked)
            at = pl.ds(pl.multiple_of(step * pair * LANE, LANE), pair * LANE)
            factor = turned_ref[r * quarter : (r + 1) * quarter, at]
            scaled = jnp.concatenate([near(waves[:quarter] * factor), near(waves[quarter:] * factor)], axis=0)
            mesh = dot(back_ref[r], scaled)
            back.append((mesh[:quarter], mesh[quarter:]))
        er, ei = back[0][0] + back[2][0], back[0][1] + back[2][1]
        fr, fi = back[0][0] - back[2][0], back[0][1] - back[2][1]
        ur, ui = back[1][0] + back[3][0], back[1][1] + back[3][1]
        vr, vi = back[1][0] - back[3][0], back[1][1] - back[3][1]
        quarters = [
            (near(er + ur), near(ei + ui)),
            (near(fr - vi), near(fi + vr)),
            (near(er - ur), near(ei - ui)),
            (near(fr + vi), near(fi - vr)),
        ]
        for part in range(2):
            for h in range(pair):
                columns = []
                for g in range(groups):
                    blocks = []
                    for t in range(tiles):
                        for m in range(4):
                            at = (g * tiles + t) * piece
                            blocks.append(quarters[m][part][at : at + piece, h * LANE : (h + 1) * LANE])
                    columns.append(jnp.concatenate(blocks, axis=0))
                spread_out = dot(jnp.concatenate(columns, axis=1), swap)
                for u in range(groups):
                    k = (step * pair + h) * groups + u
                    for t in range(tiles):
                        p_ref[part, t, pl.ds(k, tall, stride=drift), :] = spread_out[
                            t * tall : (t + 1) * tall, u * LANE : (u + 1) * LANE
                        ]
        return carry

    lax.fori_loop(0, kx // (pair * groups), transform, 0)

    def gather(i, carry):
        c = (slab + i + 1) % slabs
        rec = load(c)
        spot, cell = cells(rec)
        z_ref[0] = place(spline_weights(rec[3:4]), cell, 16)
        z_ref[1] = place(spline_slopes(rec[3:4]), cell, 16)
        y_low = [y_ref[c, part] for part in range(2)]
        slopes = [[], []]
        for z in range(spots):
            here = jnp.broadcast_to(jnp.where(spot == z, 1.0, 0.0), (ky, width)).astype(low_type)
            for part in range(2):
                slopes[part].append(y_low[part] * here)
        slope_spots = jnp.concatenate(slopes[0] + slopes[1], axis=0)
        following = (c + 1) % slabs
        planes_of = []
        for part in range(2):

            def plane(t, slab_of, z):
                return p_ref[part, t, pl.ds(pl.multiple_of((slab_of * fine + z) * drift, 8), kx), :]

            mains = [jnp.concatenate([plane(t, c, z) for t in range(tiles)], axis=1) for z in range(fine)]
            extras = [
                jnp.concatenate([mains[z][:, ky:], plane(0, following, z)[:, :ky]], axis=1)
                for z in range(REACH - 1)
            ]
            planes_of.append(near(jnp.concatenate(mains + extras, axis=0)))
        lefts = (
            jnp.concatenate([planes_of[0], planes_of[1]], axis=1),
            jnp.concatenate([planes_of[1], -planes_of[0]], axis=1),
        )
        totals = [jnp.zeros((kx, width), f32)] * 4
        for part in range(2):
            level = dot(lefts[part], spots_ref[c])
            slope = dot(lefts[part], slope_spots)
            q = qd = qz = None
            for z in range(reach):
                w = z_ref[0, z : z + 1]
                d = z_ref[1, z : z + 1]
                here = level[z * kx : (z + 1) * kx]
                there = slope[z * kx : (z + 1) * kx]
                q = here * w if q is None else q + here * w
                qz = here * d if qz is None else qz + here * d
                qd = there * w if qd is None else qd + there * w
            x, dx = x_ref[c, part], x_ref[c, 2 + part]
            totals = [totals[0] + x * q, totals[1] + dx * q, totals[2] + x * qd, totals[3] + x * qz]
        terms = jnp.concatenate([jnp.sum(t, axis=0, keepdims=True) for t in totals], axis=0)
        for j in range(grp):
            at = c * grp + j
            terms_ref[at] = terms[:, j * atoms : (j + 1) * atoms]

            @pl.when(at == me)
            def _():
                pltpu.make_async_copy(terms_ref.at[at], held_ref.at[me], got_terms).start()

            @pl.when(at != me)
            def _():
                pltpu.make_async_remote_copy(
                    src_ref=terms_ref.at[at],
                    dst_ref=held_ref.at[me],
                    send_sem=sent_terms,
                    recv_sem=got_terms,
                    device_id=(j, c),
                    device_id_type=pl.DeviceIdType.MESH,
                ).start()

        return carry

    lax.fori_loop(0, slabs, gather, 0)
    all_sent(held_ref, total_slots, got_terms)
    all_sent(held_ref, total_slots - 1, sent_terms)
    all_sent(atoms_ref, total_slots - 1, sent)
    factors = jnp.concatenate([live, loaded, loaded, loaded], axis=0)
    out_ref[...] = jnp.sum(held_ref[...], axis=0) * factors


def ring_of(slabs, groups):
    total = slabs * groups
    me = lax.axis_index("pme") * groups + lax.axis_index("grp")

    def peer(i):
        at = (me + i) % total
        return at, {
            "device_id": (at % groups, at // groups),
            "device_id_type": pl.DeviceIdType.MESH,
        }

    return me, total, peer


def meet(total, peer):
    barrier = pltpu.get_barrier_semaphore()

    def signal(i, carry):
        pl.semaphore_signal(barrier, inc=1, **peer(i)[1])
        return carry

    lax.fori_loop(1, total, signal, 0)
    return lambda: pl.semaphore_wait(barrier, total - 1)


def all_sent(ref, total, sem):
    part = ref.at[pl.ds(0, total)]
    pltpu.make_async_copy(part, part, sem).wait()


def live_of(counts_ref, shape):
    return jnp.where(lax.broadcasted_iota(jnp.int32, shape, 1) < counts_ref[0], 1.0, 0.0)


def body(slabs, groups, charge, base, frac, counts, green):
    atoms = charge.shape[0]
    kx, ky, nz = green.shape
    ny = ky * slabs
    planes = nz // slabs
    if fits(kx, ky, planes, slabs, atoms, FINE):
        return slab_body(slabs, groups, FINE, charge, base, frac, counts, green)
    slots = slabs * groups
    per = math.gcd(groups, 4)
    chunks = slots // per
    smem = pl.BlockSpec(memory_space=pltpu.SMEM)
    vmem = pl.BlockSpec(memory_space=VMEM)
    free = pl.BlockSpec(memory_space=pl.ANY)
    dma = pltpu.SemaphoreType.DMA
    index = np.arange(nz // 2)
    waves = np.stack([2 * index, 2 * index + 1])
    angle = (index[None, :, None] * waves[:, None, :] % nz) * (2.0 * math.pi / nz)
    cosine = np.cos(angle).astype(ml_dtypes.bfloat16)
    sine = np.sin(angle).astype(ml_dtypes.bfloat16)
    count = kx * ky
    width = per * atoms
    low_type = jnp.bfloat16
    wide = ky % 16 == 0
    return pl.pallas_call(
        functools.partial(mesh_kernel, (kx, ky, nz, ny, planes, groups, per, chunks, slabs)),
        out_shape=jax.ShapeDtypeStruct((4, atoms), jnp.float32),
        in_specs=[smem] + [vmem] * 3 + [free] * 3,
        out_specs=vmem,
        scratch_shapes=[
            VMEM((8, atoms), jnp.float32),
            VMEM((slots, 8, atoms), jnp.float32),
            VMEM((slots, 4, atoms), jnp.float32),
            VMEM((slots, 4, atoms), jnp.float32),
            VMEM((count, nz), jnp.float32),
            VMEM((2, nz // 2, nz // 2), low_type),
            VMEM((2, nz // 2, nz // 2), low_type),
            VMEM((chunks, 2 * count, width), low_type),
            VMEM((2 * count, width), low_type),
            VMEM((nz // LANE, 2 * count, LANE), jnp.float32),
            VMEM((2 * count, width), low_type),
            VMEM((nz + 16, 2 * count), low_type),
            VMEM((chunks, 4, kx, width) if wide else (1, 4, 8, LANE), jnp.float32),
            VMEM((chunks, 4, ky, width) if wide else (1, 4, 8, LANE), low_type),
            dma,
            dma((slabs,)),
            dma,
            dma,
            dma((3,)),
        ],
        compiler_params=pltpu.CompilerParams(
            collective_id=1, has_side_effects=True, vmem_limit_bytes=60 * 1024 * 1024
        ),
    )(counts, charge.reshape(1, atoms), frac, base, green.reshape(count, nz), cosine, sine)

def turns_of(nz, planes, fine, groups, tiles, fewer):
    quarter = nz // 4
    g, t, p, z = np.meshgrid(
        np.arange(groups), np.arange(tiles), np.arange(fewer), np.arange(fine), indexing="ij"
    )
    place_of = (p * planes + (t * groups + g) * fine + z).reshape(-1)
    ahead = []
    for r in range(4):
        wave = 4 * np.arange(quarter) + r
        angle = (wave[:, None] * place_of[None, :] % nz) * (2.0 * math.pi / nz)
        cosine, sine = np.cos(angle), np.sin(angle)
        ahead.append(np.block([[cosine, sine], [-sine, cosine]]))
    ahead = np.stack(ahead)
    return ahead.astype(ml_dtypes.bfloat16), ahead.transpose(0, 2, 1).astype(ml_dtypes.bfloat16)


def fits(kx, ky, planes, slabs, atoms, fine):
    if ky % 16 or LANE % ky or kx % 16 or slabs % 4 or planes % fine or atoms % LANE:
        return False
    groups = LANE // ky
    return (
        (planes // fine) % groups == 0
        and kx % (2 * groups) == 0
        and (slabs // 4 * fine) % 16 == 0
        and fine % 8 == 0
        and fine + REACH - 1 <= 16
    )


def slab_body(slabs, groups, fine, charge, base, frac, counts, green):
    atoms = charge.shape[0]
    kx, ky, nz = green.shape
    ny = ky * slabs
    planes = nz // slabs
    slots = slabs * groups
    width = groups * atoms
    count = kx * ky
    spots = planes // fine
    sets = LANE // ky
    tiles = spots // sets
    ahead, back = turns_of(nz, planes, fine, sets, tiles, slabs // 4)
    smem = pl.BlockSpec(memory_space=pltpu.SMEM)
    vmem = pl.BlockSpec(memory_space=VMEM)
    free = pl.BlockSpec(memory_space=pl.ANY)
    dma = pltpu.SemaphoreType.DMA
    low_type = jnp.bfloat16
    f32 = jnp.float32
    tall = slabs * fine
    return pl.pallas_call(
        functools.partial(slab_kernel, (kx, ky, nz, ny, planes, groups, slabs, fine)),
        out_shape=jax.ShapeDtypeStruct((4, atoms), f32),
        in_specs=[smem] + [vmem] * 3 + [free] * 3,
        out_specs=vmem,
        scratch_shapes=[
            VMEM((8, atoms), f32),
            VMEM((slots, 8, atoms), f32),
            VMEM((slots, 4, atoms), f32),
            VMEM((slots, 4, atoms), f32),
            VMEM((count, nz), f32),
            VMEM((nz, count), f32),
            VMEM(ahead.shape, low_type),
            VMEM(back.shape, low_type),
            VMEM((2, tiles, kx * (tall + PAD), LANE), f32),
            VMEM((2, tiles, tall * (kx + PAD), LANE), f32),
            VMEM((slabs, 4, kx, width), f32),
            VMEM((slabs, 2, ky, width), low_type),
            VMEM((slabs, 2 * spots * ky, width), low_type),
            VMEM((2, 16, width), f32),
            dma,
            dma((slabs,)),
            dma,
            dma,
            dma((3,)),
        ],
        compiler_params=pltpu.CompilerParams(
            collective_id=2, has_side_effects=True, vmem_limit_bytes=60 * 1024 * 1024
        ),
    )(counts, charge.reshape(1, atoms), frac, base, green.reshape(count, nz), ahead, back)


def solution(mesh):
    placed = (
        P(("grp", "pme")),
        P(None, ("grp", "pme")),
        P(None, ("grp", "pme")),
        P(("grp", "pme")),
        P("grp", "pme", None),
    )
    return jax.shard_map(
        functools.partial(body, mesh.shape["pme"], mesh.shape["grp"]),
        mesh=mesh,
        in_specs=placed,
        out_specs=P(None, ("grp", "pme")),
        check_vma=False,
    )
```

```python
import functools
import math

import jax
import jax.numpy as jnp
import ml_dtypes
import numpy as np
from jax import lax
from jax.experimental import pallas as pl
from jax.experimental.pallas import tpu as pltpu
from jax.sharding import PartitionSpec as P

NX = 256
LANE = 128
REACH = 4
FINE = 16
PAD = 8
VMEM = pltpu.VMEM


def spline_weights(u):
    v = 1.0 - u
    u2 = u * u
    u3 = u2 * u
    return (
        v * v * v / 6.0,
        (3.0 * u3 - 6.0 * u2 + 4.0) / 6.0,
        (-3.0 * u3 + 3.0 * u2 + 3.0 * u + 1.0) / 6.0,
        u3 / 6.0,
    )


def spline_slopes(u):
    v = 1.0 - u
    u2 = u * u
    return (
        -v * v / 2.0,
        (3.0 * u2 - 4.0 * u) / 2.0,
        (-3.0 * u2 + 2.0 * u + 1.0) / 2.0,
        u2 / 2.0,
    )


def turn_parts(turns):
    x = (turns - jnp.floor(turns + 0.5)) * math.pi
    y = x * x
    s = 1.0 / 362880.0 - y * (1.0 / 39916800.0)
    s = -1.0 / 5040.0 + y * s
    s = 1.0 / 120.0 + y * s
    s = -1.0 / 6.0 + y * s
    s = x + x * (y * s)
    c = -1.0 / 3628800.0 + y * (1.0 / 479001600.0)
    c = 1.0 / 40320.0 + y * c
    c = -1.0 / 720.0 + y * c
    c = 1.0 / 24.0 + y * c
    c = -0.5 + y * c
    c = 1.0 + y * c
    return (1.0 - 2.0 * s * s, 2.0 * s * c)


def waves_of(weight_sets, cell, waves, steps):
    copies = cell.shape[1] // waves.shape[1]

    def widen(v):
        return jnp.concatenate([v] * copies, axis=1)

    cb, sb = turn_parts(widen(waves) * cell)
    cosines = [widen(c) for c, _ in steps]
    sines = [widen(s) for _, s in steps]
    out = []
    for w in weight_sets:
        gr = w[0] + sum(w[j + 1] * cosines[j] for j in range(REACH - 1))
        gi = sum(w[j + 1] * sines[j] for j in range(REACH - 1))
        out.append((cb * gr - sb * gi, -(cb * gi + sb * gr)))
    return out


def low(values):
    return values.astype(jnp.bfloat16).astype(jnp.float32)


def place(weights, cell, rows):
    z = lax.broadcasted_iota(jnp.int32, (rows, cell.shape[1]), 0) - cell
    total = jnp.where(z == 0, weights[0], 0.0)
    for j in range(1, REACH):
        total = jnp.where(z == j, weights[j], total)
    return total


def mesh_kernel(
    dims, counts_ref, charge_ref, frac_ref, base_ref, green_in, cos_in, sin_in, out_ref,
    mine_ref, atoms_ref, terms_ref, held_ref, green_ref, cos_ref, sin_ref,
    a_ref, b_ref, s_ref, h_ref, p_ref, x_ref, y_ref, sent, got, sent_terms, got_terms, staged
):
    kx, ky, nz, ny, planes, grp, per, chunks, slabs = dims
    group, slab = lax.axis_index("grp"), lax.axis_index("pme")
    me, total_slots, peer = ring_of(slabs, grp)
    wait = meet(total_slots, peer)
    stages = [
        pltpu.make_async_copy(source, target, staged.at[i])
        for i, (source, target) in enumerate(
            [(green_in, green_ref), (cos_in, cos_ref), (sin_in, sin_ref)]
        )
    ]
    for stage in stages:
        stage.start()
    live = live_of(counts_ref, charge_ref.shape)
    loaded = charge_ref[...] * live
    mine_ref[...] = jnp.concatenate(
        [loaded, frac_ref[...], base_ref[...].astype(jnp.float32), live], axis=0
    )
    own = pltpu.make_async_copy(mine_ref, atoms_ref.at[me], got.at[slab])
    own.start()
    count = kx * ky
    width = per * LANE
    tiles = nz // LANE
    fine = min(64, LANE)
    rows = fine + 16
    wide = ky % 16 == 0

    if wide:
        xk = lax.broadcasted_iota(jnp.int32, (kx, LANE), 0)
        yk = lax.broadcasted_iota(jnp.int32, (ky, LANE), 0)
    else:
        index = lax.broadcasted_iota(jnp.int32, (count, LANE), 0)
        xk, yk = index // ky, index % ky
    xk = (xk + group * kx).astype(jnp.float32) * (1.0 / NX)
    yk = (yk + slab * ky).astype(jnp.float32) * (1.0 / ny)
    x_steps = [turn_parts(xk * j) for j in range(1, REACH)]
    y_steps = [turn_parts(yk * j) for j in range(1, REACH)]

    s_ref[...] = jnp.zeros_like(s_ref)
    dot = functools.partial(jnp.dot, preferred_element_type=jnp.float32)
    half = nz // 2
    scale = 1.0 / (ny * nz)
    for stage in stages:
        stage.wait()
    lane_in = lax.broadcasted_iota(jnp.int32, (nz, nz), 0)
    lane_out = lax.broadcasted_iota(jnp.int32, (nz, nz), 1)
    wanted = jnp.where(lane_out < half, 2 * lane_out, 2 * (lane_out - half) + 1)
    order = jnp.where(lane_in == wanted, 1.0, 0.0).astype(jnp.bfloat16)
    block = min(256, count)
    for k in range(0, count, block):
        whole = green_ref[k : k + block] * scale
        high = whole.astype(jnp.bfloat16)
        rest = (whole - high.astype(jnp.float32)).astype(jnp.bfloat16)
        green_ref[k : k + block] = dot(high, order) + dot(rest, order)
    wait()

    def send(i, carry):
        pltpu.make_async_remote_copy(
            src_ref=mine_ref,
            dst_ref=atoms_ref.at[me],
            send_sem=sent,
            recv_sem=got.at[slab],
            **peer(i)[1],
        ).start()
        return carry

    lax.fori_loop(1, total_slots, send, 0)
    share = grp // per

    def turn_to(i, ahead):
        return (slab + ahead + i // share) % slabs * share + i % share

    def load(c):
        return jnp.concatenate([atoms_ref[c * per + i] for i in range(per)], axis=1)

    def tables(rec):
        fx, fy = rec[1:2], rec[2:3]
        wx = [spline_weights(fx), spline_slopes(fx)]
        wy = [[low(w) for w in spline_weights(fy)], [low(w) for w in spline_slopes(fy)]]
        return waves_of(wx, rec[4:5], xk, x_steps), waves_of(wy, rec[5:6], yk, y_steps)

    def keep(c, rec):
        for kind, (x, y) in enumerate(zip(*tables(rec))):
            for part in range(2):
                x_ref[c, 2 * kind + part] = x[part]
                y_ref[c, 2 * kind + part] = y[part].astype(jnp.bfloat16)

    def row_of(c, kind, i):
        return [
            jnp.broadcast_to(x_ref[c, 2 * kind + part, i : i + 1], (16, width)).astype(jnp.bfloat16)
            for part in range(2)
        ]

    def product(ref, lead, c, x_kind, y_kind, made):
        if not wide:
            (xr, xi), (yr, yi) = made[0][x_kind], made[1][y_kind]
            ref[lead + (slice(0, count),)] = (xr * yr - xi * yi).astype(jnp.bfloat16)
            ref[lead + (slice(count, 2 * count),)] = (xr * yi + xi * yr).astype(jnp.bfloat16)
            return
        for i in range(kx):
            row = row_of(c, x_kind, i)
            for j in range(0, ky, 16):
                yr = y_ref[c, 2 * y_kind, j : j + 16]
                yi = y_ref[c, 2 * y_kind + 1, j : j + 16]
                at = i * ky + j
                ref[lead + (slice(at, at + 16),)] = row[0] * yr - row[1] * yi
                ref[lead + (slice(count + at, count + at + 16),)] = row[0] * yi + row[1] * yr

    def arrive(i):
        c = turn_to(i, 0)

        @pl.when(i % share == 0)
        def _():
            part = atoms_ref.at[pl.ds(c * per, grp)]
            pltpu.make_async_copy(part, part, got.at[c // share]).wait()

        return c

    def spread(i, carry):
        c = arrive(i)
        rec = load(c)
        start = (c * per) // grp * planes
        tile = start // LANE
        cell = rec[6:7].astype(jnp.int32) + (start - tile * LANE)
        wz = [rec[0:1] * w for w in spline_weights(rec[3:4])]
        table = place(wz, cell, LANE + 16).astype(jnp.bfloat16)
        rest = jnp.zeros((LANE - 16, width), jnp.bfloat16)
        table = jnp.concatenate([table, rest], axis=0)
        following = lax.rem(tile + 1, tiles)

        def add(at, size, block):
            part = lax.dot_general(
                block, table, (((1,), (1,)), ((), ())), preferred_element_type=jnp.float32
            )
            s_ref[tile, at : at + size] += part[:, :LANE]
            s_ref[following, at : at + size] += part[:, LANE:]

        if not wide:
            product(a_ref, (c,), c, 0, 0, tables(rec))
            add(0, 2 * count, a_ref[c])
            return carry
        keep(c, rec)
        some = max(1, 256 // ky)
        for i0 in range(0, kx, some):
            blocks = ([], [])
            for k in range(i0, min(i0 + some, kx)):
                row = row_of(c, 0, k)
                for j in range(0, ky, 16):
                    yr, yi = y_ref[c, 0, j : j + 16], y_ref[c, 1, j : j + 16]
                    blocks[0].append(row[0] * yr - row[1] * yi)
                    blocks[1].append(row[0] * yi + row[1] * yr)
            for part in range(2):
                block = jnp.concatenate(blocks[part], axis=0)
                at, size = part * count + i0 * ky, block.shape[0]
                a_ref[c, at : at + size] = block
                add(at, size, block)
        return carry

    lax.fori_loop(0, chunks, spread, 0)

    def dot_t(a, b):
        return lax.dot_general(a, b, (((1,), (1,)), ((), ())), preferred_element_type=jnp.float32)

    def near(values):
        return values.astype(jnp.bfloat16)

    middle = tiles // 2
    for k in range(0, count, block):
        back = []
        parts = []
        for at in (k, count + k):
            first = jnp.concatenate([s_ref[t, at : at + block] for t in range(middle)], axis=1)
            last = jnp.concatenate([s_ref[t, at : at + block] for t in range(middle, tiles)], axis=1)
            parts.append((near(first + last), near(first - last)))
        for odd in range(2):
            cosine, sine = cos_ref[odd], sin_ref[odd]
            sr, si = parts[0][odd], parts[1][odd]
            factor = green_ref[k : k + block, odd * half : (odd + 1) * half]
            hr = near((dot(sr, cosine) + dot(si, sine)) * factor)
            hi = near((dot(si, cosine) - dot(sr, sine)) * factor)
            back.append((dot_t(cosine, hr) - dot_t(sine, hi), dot_t(cosine, hi) + dot_t(sine, hr)))
        for part, at in enumerate((k, count + k)):
            even, odd = back[0][part], back[1][part]
            lower = near(even + odd)
            p_ref[0:half, at : at + block] = lower
            p_ref[half:nz, at : at + block] = near(even - odd)
            p_ref[nz : nz + 16, at : at + block] = lower[0:16]

    def gather(i, carry):
        c = turn_to(i, 1)
        rec = load(c)
        made = None if wide else tables(rec)
        product(b_ref, (), c, 1, 0, made)
        product(h_ref, (), c, 0, 1, made)
        start = (c * per) // grp * planes
        base = start // fine * fine
        cell = rec[6:7].astype(jnp.int32) + (start - base)
        window = p_ref[pl.ds(pl.multiple_of(base, 16), rows), :]
        level = dot(window, a_ref[c])
        along_x = dot(window, b_ref[...])
        along_y = dot(window, h_ref[...])
        wz = place(spline_weights(rec[3:4]), cell, rows)
        dz = place(spline_slopes(rec[3:4]), cell, rows)

        def total(values):
            return jnp.sum(values, axis=0, keepdims=True)

        terms = jnp.concatenate(
            [total(wz * level), total(wz * along_x), total(wz * along_y), total(dz * level)], axis=0
        )
        for j in range(per):
            at = c * per + j
            terms_ref[at] = terms[:, j * LANE : (j + 1) * LANE]

            @pl.when(at == me)
            def _():
                pltpu.make_async_copy(terms_ref.at[at], held_ref.at[me], got_terms).start()

            @pl.when(at != me)
            def _():
                pltpu.make_async_remote_copy(
                    src_ref=terms_ref.at[at],
                    dst_ref=held_ref.at[me],
                    send_sem=sent_terms,
                    recv_sem=got_terms,
                    device_id=(at % grp, at // grp),
                    device_id_type=pl.DeviceIdType.MESH,
                ).start()

        return carry

    lax.fori_loop(0, chunks, gather, 0)
    all_sent(held_ref, total_slots, got_terms)
    all_sent(held_ref, total_slots - 1, sent_terms)
    all_sent(atoms_ref, total_slots - 1, sent)
    factors = jnp.concatenate([live, loaded, loaded, loaded], axis=0)
    out_ref[...] = jnp.sum(held_ref[...], axis=0) * factors

def digits(value, radix):
    return value // radix, value % radix


def waves_by_parts(weight_sets, cell, first, unit, steps):
    width = cell.shape[1]
    count = steps[0][0].shape[0]
    copies = width // LANE
    low_rows = lax.broadcasted_iota(jnp.int32, (8, width), 0)
    fine_c, fine_s = turn_parts(low_rows.astype(jnp.float32) * unit * cell)
    coarse_rows = (first + 8 * low_rows).astype(jnp.float32) * unit
    coarse_c, coarse_s = turn_parts(coarse_rows * cell)

    def widen(v):
        return jnp.concatenate([v] * copies, axis=1)

    cosines = [widen(c) for c, _ in steps]
    sines = [widen(s) for _, s in steps]
    turned = []
    for i in range(count // 8):
        c, s = coarse_c[i : i + 1], coarse_s[i : i + 1]
        turned.append((c * fine_c - s * fine_s, s * fine_c + c * fine_s))
    cb = jnp.concatenate([c for c, _ in turned], axis=0)
    sb = jnp.concatenate([s for _, s in turned], axis=0)
    out = []
    for w in weight_sets:
        gr = w[0] + sum(w[j + 1] * cosines[j] for j in range(REACH - 1))
        gi = sum(w[j + 1] * sines[j] for j in range(REACH - 1))
        out.append((cb * gr - sb * gi, -(cb * gi + sb * gr)))
    return out


def slab_kernel(
    dims, counts_in, charge_in, frac_in, base_in, green_in, ahead_in, back_in, out_ref,
    counts_ref, charge_ref, frac_ref, base_ref,
    mine_ref, atoms_ref, terms_ref, held_ref, green_ref, turned_ref, ahead_ref, back_ref,
    s_ref, p_ref, x_ref, y_ref, spots_ref, z_ref, hot_ref,
    left_0, left_1, right_0, right_1, sent, got, sent_terms, got_terms, staged
):
    kx, ky, nz, ny, planes, grp, slabs, fine = dims
    group, slab = lax.axis_index("grp"), lax.axis_index("pme")
    me, total_slots, peer = ring_of(slabs, grp)
    wait = meet(total_slots, peer)
    stages = [
        pltpu.make_async_copy(source, target, staged.at[i])
        for i, (source, target) in enumerate(
            [
                (counts_in, counts_ref),
                (charge_in, charge_ref),
                (frac_in, frac_ref),
                (base_in, base_ref),
                (green_in, green_ref),
                (ahead_in, ahead_ref),
                (back_in, back_ref),
            ]
        )
    ]
    for stage in stages:
        stage.start()
    for stage in stages[:4]:
        stage.wait()
    live = live_of(counts_ref, charge_ref.shape)
    loaded = charge_ref[...] * live
    mine_ref[...] = jnp.concatenate(
        [loaded, frac_ref[...], base_ref[...].astype(jnp.float32), live], axis=0
    )
    own = pltpu.make_async_copy(mine_ref, atoms_ref.at[me], got.at[slab])
    own.start()

    atoms = charge_ref.shape[1]
    width = grp * atoms
    groups = LANE // ky
    spots = planes // fine
    tiles = spots // groups
    lanes = spots * ky
    reach = fine + REACH - 1
    tall = slabs * fine
    pitch = tall + PAD
    drift = kx + PAD
    quarter = nz // 4
    low_type = jnp.bfloat16
    f32 = jnp.float32
    left_refs, right_refs = (left_0, left_1), (right_0, right_1)
    dot = functools.partial(jnp.dot, preferred_element_type=f32)

    def dot_t(a, b):
        return lax.dot_general(a, b, (((1,), (1,)), ((), ())), preferred_element_type=f32)

    xk = (lax.broadcasted_iota(jnp.int32, (kx, LANE), 0) + group * kx).astype(f32) * (1.0 / NX)
    yk = (lax.broadcasted_iota(jnp.int32, (ky, LANE), 0) + slab * ky).astype(f32) * (1.0 / ny)
    x_steps = [turn_parts(xk * j) for j in range(1, REACH)]
    y_steps = [turn_parts(yk * j) for j in range(1, REACH)]

    for part in range(2):
        for t in range(tiles):
            for z in range(REACH - 1):
                for p in range(slabs):
                    s_ref[part, t, pl.ds(p * fine + z, kx, stride=pitch), :] = jnp.zeros((kx, LANE), f32)
    for stage in stages[4:]:
        stage.wait()
    row = lax.broadcasted_iota(jnp.int32, (nz, nz), 0)
    column = lax.broadcasted_iota(jnp.int32, (nz, nz), 1)
    wanted = 4 * (row % quarter) + row // quarter
    order = jnp.where(column == wanted, 1.0, 0.0).astype(low_type)
    scale = 1.0 / (ny * nz)
    block = 2 * LANE
    for k in range(0, kx * ky, block):
        whole = green_ref[k : k + block] * scale
        high = whole.astype(low_type)
        rest = (whole - high.astype(f32)).astype(low_type)
        turned_ref[:, k : k + block] = dot_t(order, high) + dot_t(order, rest)
    wait()

    def send(i, carry):
        pltpu.make_async_remote_copy(
            src_ref=mine_ref,
            dst_ref=atoms_ref.at[me],
            send_sem=sent,
            recv_sem=got.at[slab],
            **peer(i)[1],
        ).start()
        return carry

    lax.fori_loop(1, total_slots, send, 0)

    def load(c):
        return jnp.concatenate([atoms_ref[c * grp + i] for i in range(grp)], axis=1)

    def cells(rec):
        cell = rec[6:7].astype(jnp.int32)
        return digits(cell, fine)

    def tile_of(row):
        return jnp.broadcast_to(row, (16, width)).astype(low_type)

    def hot_rows(spot):
        return jnp.where(lax.broadcasted_iota(jnp.int32, (spots, width), 0) == spot, 1.0, 0.0)

    def arrive(i):
        c = (slab + i) % slabs
        part = atoms_ref.at[pl.ds(c * grp, grp)]
        pltpu.make_async_copy(part, part, got.at[c]).wait()

    def build(i, side_of):
        c = (slab + i) % slabs
        rec = load(c)
        fx, fy, fz = rec[1:2], rec[2:3], rec[3:4]
        wx = [spline_weights(fx), spline_slopes(fx)]
        wy = [[low(w) for w in spline_weights(fy)], [low(w) for w in spline_slopes(fy)]]
        xs = waves_by_parts(wx, rec[4:5], group * kx, 1.0 / NX, x_steps)
        ys = waves_by_parts(wy, rec[5:6], slab * ky, 1.0 / ny, y_steps)
        for kind in range(2):
            for part in range(2):
                x_ref[c, 2 * kind + part] = xs[kind][part]
        for part in range(2):
            y_ref[c, part] = ys[1][part].astype(low_type)
        spot, cell = cells(rec)
        y_low = [ys[0][part].astype(low_type) for part in range(2)]
        hot_ref[side_of] = hot_rows(spot)
        for z in range(spots):
            here = tile_of(hot_ref[side_of, z : z + 1])
            for part in range(2):
                for j in range(0, ky, 16):
                    at = part * lanes + z * ky + j
                    made = y_low[part][j : j + 16] * here
                    spots_ref[c, at : at + 16] = made
                    right_refs[side_of][at : at + 16] = made
        z_ref[side_of] = place(spline_weights(fz), cell, z_ref.shape[1])
        x_low = [(xs[0][part] * rec[0:1]).astype(low_type) for part in range(2)]
        at = 0
        for z in range(reach):
            weight = tile_of(z_ref[side_of, z : z + 1])
            for part in range(2):
                for j in range(0, kx, 16):
                    left_refs[side_of][at : at + 16] = x_low[part][j : j + 16] * weight
                    at += 16

    def mix(i, side_of):
        c = (slab + i) % slabs
        made = dot_t(left_refs[side_of][...], right_refs[side_of][...])

        def mesh_rows(z):
            at = 2 * z * kx
            real, imag = made[at : at + kx], made[at + kx : at + 2 * kx]
            return (
                real[:, :lanes] - imag[:, lanes:],
                real[:, lanes:] + imag[:, :lanes],
            )

        following = (c + 1) % slabs
        first = lax.broadcasted_iota(jnp.int32, (kx, lanes), 1) < ky

        def rows_at(slab_of, z):
            return pl.ds(slab_of * fine + z, kx, stride=pitch)

        held = {}
        for z in range(REACH - 1):
            for part in range(2):
                for t in range(tiles):
                    held[z, part, t] = s_ref[part, t, rows_at(c, z), :]
                held[z, part] = s_ref[part, 0, rows_at(following, z), :]
        for z in range(fine):
            values = mesh_rows(z)
            past = mesh_rows(z + fine) if z + fine < reach else None
            for part in range(2):
                value = values[part]
                if past is not None:
                    moved = jnp.concatenate(
                        [past[part][:, lanes - ky :], past[part][:, : lanes - ky]], axis=1
                    )
                    value = value + jnp.where(first, 0.0, moved)
                    s_ref[part, 0, rows_at(following, z), :] = (
                        held[z, part] + jnp.where(first, moved, 0.0)[:, :LANE]
                    )
                for t in range(tiles):
                    out = value[:, t * LANE : (t + 1) * LANE]
                    if past is not None:
                        out = out + held[z, part, t]
                    s_ref[part, t, rows_at(c, z), :] = out

    def two(j, carry):
        arrive(2 * j + 1)
        arrive(2 * j + 2)
        mix(2 * j, 0)
        build(2 * j + 1, 1)
        mix(2 * j + 1, 1)
        build(2 * j + 2, 0)
        return carry

    arrive(0)
    build(0, 0)
    lax.fori_loop(0, slabs // 2 - 1, two, 0)
    arrive(slabs - 1)
    mix(slabs - 2, 0)
    build(slabs - 1, 1)
    mix(slabs - 1, 1)

    side = groups * LANE
    row = lax.broadcasted_iota(jnp.int32, (side, side), 0)
    column = lax.broadcasted_iota(jnp.int32, (side, side), 1)
    wanted = (row % LANE) // ky * LANE + row // LANE * ky + row % ky
    swap = jnp.where(column == wanted, 1.0, 0.0).astype(low_type)
    fewer = slabs // 4
    piece = fewer * fine
    pair = 2

    def near(values):
        return values.astype(low_type)

    def transform(step, carry):
        picked = []
        for part in range(2):
            halves = []
            for h in range(pair):
                k0 = (step * pair + h) * groups
                left = jnp.concatenate(
                    [
                        jnp.concatenate(
                            [
                                s_ref[part, t, pl.ds(pl.multiple_of((k0 + u) * pitch, 8), tall), :]
                                for u in range(groups)
                            ],
                            axis=1,
                        )
                        for t in range(tiles)
                    ],
                    axis=0,
                )
                halves.append(dot(near(left), swap))
            quarters = []
            for m in range(4):
                blocks = []
                for g in range(groups):
                    for t in range(tiles):
                        at = t * tall + m * piece
                        blocks.append(
                            jnp.concatenate(
                                [half[at : at + piece, g * LANE : (g + 1) * LANE] for half in halves], axis=1
                            )
                        )
                quarters.append(jnp.concatenate(blocks, axis=0))
            picked.append(quarters)
        re, im = picked
        ar, ai, br, bi = re[0] + re[2], im[0] + im[2], re[0] - re[2], im[0] - im[2]
        cr, ci, dr, di = re[1] + re[3], im[1] + im[3], re[1] - re[3], im[1] - im[3]
        mixed = [(ar + cr, ai + ci), (br + di, bi - dr), (ar - cr, ai - ci), (br - di, bi + dr)]
        back = []
        for r in range(4):
            stacked = jnp.concatenate([near(mixed[r][0]), near(mixed[r][1])], axis=0)
            waves = dot(ahead_ref[r], stacked)
            at = pl.ds(pl.multiple_of(step * pair * LANE, LANE), pair * LANE)
            factor = turned_ref[r * quarter : (r + 1) * quarter, at]
            scaled = jnp.concatenate([near(waves[:quarter] * factor), near(waves[quarter:] * factor)], axis=0)
            mesh = dot(back_ref[r], scaled)
            back.append((mesh[:quarter], mesh[quarter:]))
        er, ei = back[0][0] + back[2][0], back[0][1] + back[2][1]
        fr, fi = back[0][0] - back[2][0], back[0][1] - back[2][1]
        ur, ui = back[1][0] + back[3][0], back[1][1] + back[3][1]
        vr, vi = back[1][0] - back[3][0], back[1][1] - back[3][1]
        quarters = [
            (near(er + ur), near(ei + ui)),
            (near(fr - vi), near(fi + vr)),
            (near(er - ur), near(ei - ui)),
            (near(fr + vi), near(fi - vr)),
        ]
        for part in range(2):
            for h in range(pair):
                columns = []
                for g in range(groups):
                    blocks = []
                    for t in range(tiles):
                        for m in range(4):
                            at = (g * tiles + t) * piece
                            blocks.append(quarters[m][part][at : at + piece, h * LANE : (h + 1) * LANE])
                    columns.append(jnp.concatenate(blocks, axis=0))
                spread_out = dot(jnp.concatenate(columns, axis=1), swap)
                for u in range(groups):
                    k = (step * pair + h) * groups + u
                    for t in range(tiles):
                        p_ref[part, t, pl.ds(k, tall, stride=drift), :] = spread_out[
                            t * tall : (t + 1) * tall, u * LANE : (u + 1) * LANE
                        ]
        return carry

    for step in range(kx // (pair * groups)):
        transform(step, 0)

    def gather(i, carry):
        c = (slab + i + 1) % slabs
        rec = load(c)
        spot, cell = cells(rec)
        z_ref[0] = place(spline_weights(rec[3:4]), cell, z_ref.shape[1])
        z_ref[1] = place(spline_slopes(rec[3:4]), cell, z_ref.shape[1])
        y_low = [y_ref[c, part] for part in range(2)]
        slopes = [[], []]
        hot_ref[0] = hot_rows(spot)
        for z in range(spots):
            here = tile_of(hot_ref[0, z : z + 1])
            for part in range(2):
                slopes[part] += [y_low[part][j : j + 16] * here for j in range(0, ky, 16)]
        slope_spots = jnp.concatenate(slopes[0] + slopes[1], axis=0)
        following = (c + 1) % slabs
        planes_of = []
        for part in range(2):

            def plane(t, slab_of, z):
                return p_ref[part, t, pl.ds(pl.multiple_of((slab_of * fine + z) * drift, 8), kx), :]

            mains = [jnp.concatenate([plane(t, c, z) for t in range(tiles)], axis=1) for z in range(fine)]
            extras = [
                jnp.concatenate([mains[z][:, ky:], plane(0, following, z)[:, :ky]], axis=1)
                for z in range(REACH - 1)
            ]
            planes_of.append(near(jnp.concatenate(mains + extras, axis=0)))
        lefts = (
            jnp.concatenate([planes_of[0], planes_of[1]], axis=1),
            jnp.concatenate([planes_of[1], -planes_of[0]], axis=1),
        )
        totals = [jnp.zeros((kx, width), f32)] * 4
        for part in range(2):
            level = dot(lefts[part], spots_ref[c])
            slope = dot(lefts[part], slope_spots)
            q = qd = qz = None
            for z in range(reach):
                w = z_ref[0, z : z + 1]
                d = z_ref[1, z : z + 1]
                here = level[z * kx : (z + 1) * kx]
                there = slope[z * kx : (z + 1) * kx]
                q = here * w if q is None else q + here * w
                qz = here * d if qz is None else qz + here * d
                qd = there * w if qd is None else qd + there * w
            x, dx = x_ref[c, part], x_ref[c, 2 + part]
            totals = [totals[0] + x * q, totals[1] + dx * q, totals[2] + x * qd, totals[3] + x * qz]
        terms = jnp.concatenate([jnp.sum(t, axis=0, keepdims=True) for t in totals], axis=0)
        for j in range(grp):
            at = c * grp + j
            terms_ref[at] = terms[:, j * atoms : (j + 1) * atoms]

            @pl.when(at == me)
            def _():
                pltpu.make_async_copy(terms_ref.at[at], held_ref.at[me], got_terms).start()

            @pl.when(at != me)
            def _():
                pltpu.make_async_remote_copy(
                    src_ref=terms_ref.at[at],
                    dst_ref=held_ref.at[me],
                    send_sem=sent_terms,
                    recv_sem=got_terms,
                    device_id=(j, c),
                    device_id_type=pl.DeviceIdType.MESH,
                ).start()

        return carry

    lax.fori_loop(0, slabs, gather, 0)
    all_sent(held_ref, total_slots, got_terms)
    all_sent(held_ref, total_slots - 1, sent_terms)
    all_sent(atoms_ref, total_slots - 1, sent)
    factors = jnp.concatenate([live, loaded, loaded, loaded], axis=0)
    out_ref[...] = jnp.sum(held_ref[...], axis=0) * factors


def ring_of(slabs, groups):
    total = slabs * groups
    me = lax.axis_index("pme") * groups + lax.axis_index("grp")

    def peer(i):
        at = (me + i) % total
        return at, {
            "device_id": (at % groups, at // groups),
            "device_id_type": pl.DeviceIdType.MESH,
        }

    return me, total, peer


def meet(total, peer):
    barrier = pltpu.get_barrier_semaphore()

    def signal(i, carry):
        pl.semaphore_signal(barrier, inc=1, **peer(i)[1])
        return carry

    lax.fori_loop(1, total, signal, 0)
    return lambda: pl.semaphore_wait(barrier, total - 1)


def all_sent(ref, total, sem):
    part = ref.at[pl.ds(0, total)]
    pltpu.make_async_copy(part, part, sem).wait()


def live_of(counts_ref, shape):
    return jnp.where(lax.broadcasted_iota(jnp.int32, shape, 1) < counts_ref[0], 1.0, 0.0)


def body(slabs, groups, charge, base, frac, counts, green):
    atoms = charge.shape[0]
    kx, ky, nz = green.shape
    ny = ky * slabs
    planes = nz // slabs
    if fits(kx, ky, planes, slabs, atoms, FINE):
        return slab_body(slabs, groups, FINE, charge, base, frac, counts, green)
    slots = slabs * groups
    per = math.gcd(groups, 4)
    chunks = slots // per
    smem = pl.BlockSpec(memory_space=pltpu.SMEM)
    vmem = pl.BlockSpec(memory_space=VMEM)
    free = pl.BlockSpec(memory_space=pl.ANY)
    dma = pltpu.SemaphoreType.DMA
    index = np.arange(nz // 2)
    waves = np.stack([2 * index, 2 * index + 1])
    angle = (index[None, :, None] * waves[:, None, :] % nz) * (2.0 * math.pi / nz)
    cosine = np.cos(angle).astype(ml_dtypes.bfloat16)
    sine = np.sin(angle).astype(ml_dtypes.bfloat16)
    count = kx * ky
    width = per * atoms
    low_type = jnp.bfloat16
    wide = ky % 16 == 0
    return pl.pallas_call(
        functools.partial(mesh_kernel, (kx, ky, nz, ny, planes, groups, per, chunks, slabs)),
        out_shape=jax.ShapeDtypeStruct((4, atoms), jnp.float32),
        in_specs=[smem] + [vmem] * 3 + [free] * 3,
        out_specs=vmem,
        scratch_shapes=[
            VMEM((8, atoms), jnp.float32),
            VMEM((slots, 8, atoms), jnp.float32),
            VMEM((slots, 4, atoms), jnp.float32),
            VMEM((slots, 4, atoms), jnp.float32),
            VMEM((count, nz), jnp.float32),
            VMEM((2, nz // 2, nz // 2), low_type),
            VMEM((2, nz // 2, nz // 2), low_type),
            VMEM((chunks, 2 * count, width), low_type),
            VMEM((2 * count, width), low_type),
            VMEM((nz // LANE, 2 * count, LANE), jnp.float32),
            VMEM((2 * count, width), low_type),
            VMEM((nz + 16, 2 * count), low_type),
            VMEM((chunks, 4, kx, width) if wide else (1, 4, 8, LANE), jnp.float32),
            VMEM((chunks, 4, ky, width) if wide else (1, 4, 8, LANE), low_type),
            dma,
            dma((slabs,)),
            dma,
            dma,
            dma((3,)),
        ],
        compiler_params=pltpu.CompilerParams(
            collective_id=1, has_side_effects=True, vmem_limit_bytes=60 * 1024 * 1024
        ),
    )(counts, charge.reshape(1, atoms), frac, base, green.reshape(count, nz), cosine, sine)

def turns_of(nz, planes, fine, groups, tiles, fewer):
    quarter = nz // 4
    g, t, p, z = np.meshgrid(
        np.arange(groups), np.arange(tiles), np.arange(fewer), np.arange(fine), indexing="ij"
    )
    place_of = (p * planes + (t * groups + g) * fine + z).reshape(-1)
    ahead = []
    for r in range(4):
        wave = 4 * np.arange(quarter) + r
        angle = (wave[:, None] * place_of[None, :] % nz) * (2.0 * math.pi / nz)
        cosine, sine = np.cos(angle), np.sin(angle)
        ahead.append(np.block([[cosine, sine], [-sine, cosine]]))
    ahead = np.stack(ahead)
    return ahead.astype(ml_dtypes.bfloat16), ahead.transpose(0, 2, 1).astype(ml_dtypes.bfloat16)


def fits(kx, ky, planes, slabs, atoms, fine):
    if ky % 16 or LANE % ky or kx % 16 or slabs % 4 or planes % fine or atoms % LANE:
        return False
    groups = LANE // ky
    return (
        (planes // fine) % groups == 0
        and kx % (2 * groups) == 0
        and (slabs // 4 * fine) % 16 == 0
        and fine % 8 == 0
        and fine + REACH - 1 <= 24
    )


def slab_body(slabs, groups, fine, charge, base, frac, counts, green):
    atoms = charge.shape[0]
    kx, ky, nz = green.shape
    ny = ky * slabs
    planes = nz // slabs
    slots = slabs * groups
    width = groups * atoms
    count = kx * ky
    spots = planes // fine
    sets = LANE // ky
    tiles = spots // sets
    ahead, back = turns_of(nz, planes, fine, sets, tiles, slabs // 4)
    vmem = pl.BlockSpec(memory_space=VMEM)
    free = pl.BlockSpec(memory_space=pl.ANY)
    dma = pltpu.SemaphoreType.DMA
    low_type = jnp.bfloat16
    f32 = jnp.float32
    tall = slabs * fine
    reach = fine + REACH - 1
    return pl.pallas_call(
        functools.partial(slab_kernel, (kx, ky, nz, ny, planes, groups, slabs, fine)),
        out_shape=jax.ShapeDtypeStruct((4, atoms), f32),
        in_specs=[free] * 7,
        out_specs=vmem,
        scratch_shapes=[
            pltpu.SMEM((1,), jnp.int32),
            VMEM((1, atoms), f32),
            VMEM((3, atoms), f32),
            VMEM((3, atoms), jnp.int32),
            VMEM((8, atoms), f32),
            VMEM((slots, 8, atoms), f32),
            VMEM((slots, 4, atoms), f32),
            VMEM((slots, 4, atoms), f32),
            VMEM((count, nz), f32),
            VMEM((nz, count), f32),
            VMEM(ahead.shape, low_type),
            VMEM(back.shape, low_type),
            VMEM((2, tiles, kx * (tall + PAD), LANE), f32),
            VMEM((2, tiles, tall * (kx + PAD), LANE), f32),
            VMEM((slabs, 4, kx, width), f32),
            VMEM((slabs, 2, ky, width), low_type),
            VMEM((slabs, 2 * spots * ky, width), low_type),
            VMEM((2, 24, width), f32),
            VMEM((2, spots, width), f32),
            VMEM((2 * reach * kx, width), low_type),
            VMEM((2 * reach * kx, width), low_type),
            VMEM((2 * spots * ky, width), low_type),
            VMEM((2 * spots * ky, width), low_type),
            dma,
            dma((slabs,)),
            dma,
            dma,
            dma((7,)),
        ],
        compiler_params=pltpu.CompilerParams(
            collective_id=2, has_side_effects=True, vmem_limit_bytes=60 * 1024 * 1024
        ),
    )(counts, charge.reshape(1, atoms), frac, base, green.reshape(count, nz), ahead, back)


def solution(mesh):
    placed = (
        P(("grp", "pme")),
        P(None, ("grp", "pme")),
        P(None, ("grp", "pme")),
        P(("grp", "pme")),
        P("grp", "pme", None),
    )
    return jax.shard_map(
        functools.partial(body, mesh.shape["pme"], mesh.shape["grp"]),
        mesh=mesh,
        in_specs=placed,
        out_specs=P(None, ("grp", "pme")),
        check_vma=False,
    )
```

```python
import functools
import math

import jax
import jax.numpy as jnp
import ml_dtypes
import numpy as np
from jax import lax
from jax.experimental import pallas as pl
from jax.experimental.pallas import tpu as pltpu
from jax.sharding import PartitionSpec as P

NX = 256
LANE = 128
REACH = 4
FINE = 16
PAD = 8
VMEM = pltpu.VMEM


def spline_weights(u):
    v = 1.0 - u
    u2 = u * u
    u3 = u2 * u
    return (
        v * v * v / 6.0,
        (3.0 * u3 - 6.0 * u2 + 4.0) / 6.0,
        (-3.0 * u3 + 3.0 * u2 + 3.0 * u + 1.0) / 6.0,
        u3 / 6.0,
    )


def spline_slopes(u):
    v = 1.0 - u
    u2 = u * u
    return (
        -v * v / 2.0,
        (3.0 * u2 - 4.0 * u) / 2.0,
        (-3.0 * u2 + 2.0 * u + 1.0) / 2.0,
        u2 / 2.0,
    )


def turn_parts(turns):
    x = (turns - jnp.floor(turns + 0.5)) * math.pi
    y = x * x
    s = 1.0 / 362880.0 - y * (1.0 / 39916800.0)
    s = -1.0 / 5040.0 + y * s
    s = 1.0 / 120.0 + y * s
    s = -1.0 / 6.0 + y * s
    s = x + x * (y * s)
    c = -1.0 / 3628800.0 + y * (1.0 / 479001600.0)
    c = 1.0 / 40320.0 + y * c
    c = -1.0 / 720.0 + y * c
    c = 1.0 / 24.0 + y * c
    c = -0.5 + y * c
    c = 1.0 + y * c
    return (1.0 - 2.0 * s * s, 2.0 * s * c)


def waves_of(weight_sets, cell, waves, steps):
    copies = cell.shape[1] // waves.shape[1]

    def widen(v):
        return jnp.concatenate([v] * copies, axis=1)

    cb, sb = turn_parts(widen(waves) * cell)
    cosines = [widen(c) for c, _ in steps]
    sines = [widen(s) for _, s in steps]
    out = []
    for w in weight_sets:
        gr = w[0] + sum(w[j + 1] * cosines[j] for j in range(REACH - 1))
        gi = sum(w[j + 1] * sines[j] for j in range(REACH - 1))
        out.append((cb * gr - sb * gi, -(cb * gi + sb * gr)))
    return out


def low(values):
    return values.astype(jnp.bfloat16).astype(jnp.float32)


def place(weights, cell, rows):
    z = lax.broadcasted_iota(jnp.int32, (rows, cell.shape[1]), 0) - cell
    total = jnp.where(z == 0, weights[0], 0.0)
    for j in range(1, REACH):
        total = jnp.where(z == j, weights[j], total)
    return total


def mesh_kernel(
    dims, counts_ref, charge_ref, frac_ref, base_ref, green_in, cos_in, sin_in, out_ref,
    mine_ref, atoms_ref, terms_ref, held_ref, green_ref, cos_ref, sin_ref,
    a_ref, b_ref, s_ref, h_ref, p_ref, x_ref, y_ref, sent, got, sent_terms, got_terms, staged
):
    kx, ky, nz, ny, planes, grp, per, chunks, slabs = dims
    group, slab = lax.axis_index("grp"), lax.axis_index("pme")
    me, total_slots, peer = ring_of(slabs, grp)
    wait = meet(total_slots, peer)
    stages = [
        pltpu.make_async_copy(source, target, staged.at[i])
        for i, (source, target) in enumerate(
            [(green_in, green_ref), (cos_in, cos_ref), (sin_in, sin_ref)]
        )
    ]
    for stage in stages:
        stage.start()
    live = live_of(counts_ref, charge_ref.shape)
    loaded = charge_ref[...] * live
    mine_ref[...] = jnp.concatenate(
        [loaded, frac_ref[...], base_ref[...].astype(jnp.float32), live], axis=0
    )
    own = pltpu.make_async_copy(mine_ref, atoms_ref.at[me], got.at[slab])
    own.start()
    count = kx * ky
    width = per * LANE
    tiles = nz // LANE
    fine = min(64, LANE)
    rows = fine + 16
    wide = ky % 16 == 0

    if wide:
        xk = lax.broadcasted_iota(jnp.int32, (kx, LANE), 0)
        yk = lax.broadcasted_iota(jnp.int32, (ky, LANE), 0)
    else:
        index = lax.broadcasted_iota(jnp.int32, (count, LANE), 0)
        xk, yk = index // ky, index % ky
    xk = (xk + group * kx).astype(jnp.float32) * (1.0 / NX)
    yk = (yk + slab * ky).astype(jnp.float32) * (1.0 / ny)
    x_steps = [turn_parts(xk * j) for j in range(1, REACH)]
    y_steps = [turn_parts(yk * j) for j in range(1, REACH)]

    s_ref[...] = jnp.zeros_like(s_ref)
    dot = functools.partial(jnp.dot, preferred_element_type=jnp.float32)
    half = nz // 2
    scale = 1.0 / (ny * nz)
    for stage in stages:
        stage.wait()
    lane_in = lax.broadcasted_iota(jnp.int32, (nz, nz), 0)
    lane_out = lax.broadcasted_iota(jnp.int32, (nz, nz), 1)
    wanted = jnp.where(lane_out < half, 2 * lane_out, 2 * (lane_out - half) + 1)
    order = jnp.where(lane_in == wanted, 1.0, 0.0).astype(jnp.bfloat16)
    block = min(256, count)
    for k in range(0, count, block):
        whole = green_ref[k : k + block] * scale
        high = whole.astype(jnp.bfloat16)
        rest = (whole - high.astype(jnp.float32)).astype(jnp.bfloat16)
        green_ref[k : k + block] = dot(high, order) + dot(rest, order)
    wait()

    def send(i, carry):
        pltpu.make_async_remote_copy(
            src_ref=mine_ref,
            dst_ref=atoms_ref.at[me],
            send_sem=sent,
            recv_sem=got.at[slab],
            **peer(i)[1],
        ).start()
        return carry

    lax.fori_loop(1, total_slots, send, 0)
    share = grp // per

    def turn_to(i, ahead):
        return (slab + ahead + i // share) % slabs * share + i % share

    def load(c):
        return jnp.concatenate([atoms_ref[c * per + i] for i in range(per)], axis=1)

    def tables(rec):
        fx, fy = rec[1:2], rec[2:3]
        wx = [spline_weights(fx), spline_slopes(fx)]
        wy = [[low(w) for w in spline_weights(fy)], [low(w) for w in spline_slopes(fy)]]
        return waves_of(wx, rec[4:5], xk, x_steps), waves_of(wy, rec[5:6], yk, y_steps)

    def keep(c, rec):
        for kind, (x, y) in enumerate(zip(*tables(rec))):
            for part in range(2):
                x_ref[c, 2 * kind + part] = x[part]
                y_ref[c, 2 * kind + part] = y[part].astype(jnp.bfloat16)

    def row_of(c, kind, i):
        return [
            jnp.broadcast_to(x_ref[c, 2 * kind + part, i : i + 1], (16, width)).astype(jnp.bfloat16)
            for part in range(2)
        ]

    def product(ref, lead, c, x_kind, y_kind, made):
        if not wide:
            (xr, xi), (yr, yi) = made[0][x_kind], made[1][y_kind]
            ref[lead + (slice(0, count),)] = (xr * yr - xi * yi).astype(jnp.bfloat16)
            ref[lead + (slice(count, 2 * count),)] = (xr * yi + xi * yr).astype(jnp.bfloat16)
            return
        for i in range(kx):
            row = row_of(c, x_kind, i)
            for j in range(0, ky, 16):
                yr = y_ref[c, 2 * y_kind, j : j + 16]
                yi = y_ref[c, 2 * y_kind + 1, j : j + 16]
                at = i * ky + j
                ref[lead + (slice(at, at + 16),)] = row[0] * yr - row[1] * yi
                ref[lead + (slice(count + at, count + at + 16),)] = row[0] * yi + row[1] * yr

    def arrive(i):
        c = turn_to(i, 0)

        @pl.when(i % share == 0)
        def _():
            part = atoms_ref.at[pl.ds(c * per, grp)]
            pltpu.make_async_copy(part, part, got.at[c // share]).wait()

        return c

    def spread(i, carry):
        c = arrive(i)
        rec = load(c)
        start = (c * per) // grp * planes
        tile = start // LANE
        cell = rec[6:7].astype(jnp.int32) + (start - tile * LANE)
        wz = [rec[0:1] * w for w in spline_weights(rec[3:4])]
        table = place(wz, cell, LANE + 16).astype(jnp.bfloat16)
        rest = jnp.zeros((LANE - 16, width), jnp.bfloat16)
        table = jnp.concatenate([table, rest], axis=0)
        following = lax.rem(tile + 1, tiles)

        def add(at, size, block):
            part = lax.dot_general(
                block, table, (((1,), (1,)), ((), ())), preferred_element_type=jnp.float32
            )
            s_ref[tile, at : at + size] += part[:, :LANE]
            s_ref[following, at : at + size] += part[:, LANE:]

        if not wide:
            product(a_ref, (c,), c, 0, 0, tables(rec))
            add(0, 2 * count, a_ref[c])
            return carry
        keep(c, rec)
        some = max(1, 256 // ky)
        for i0 in range(0, kx, some):
            blocks = ([], [])
            for k in range(i0, min(i0 + some, kx)):
                row = row_of(c, 0, k)
                for j in range(0, ky, 16):
                    yr, yi = y_ref[c, 0, j : j + 16], y_ref[c, 1, j : j + 16]
                    blocks[0].append(row[0] * yr - row[1] * yi)
                    blocks[1].append(row[0] * yi + row[1] * yr)
            for part in range(2):
                block = jnp.concatenate(blocks[part], axis=0)
                at, size = part * count + i0 * ky, block.shape[0]
                a_ref[c, at : at + size] = block
                add(at, size, block)
        return carry

    lax.fori_loop(0, chunks, spread, 0)

    def dot_t(a, b):
        return lax.dot_general(a, b, (((1,), (1,)), ((), ())), preferred_element_type=jnp.float32)

    def near(values):
        return values.astype(jnp.bfloat16)

    middle = tiles // 2
    for k in range(0, count, block):
        back = []
        parts = []
        for at in (k, count + k):
            first = jnp.concatenate([s_ref[t, at : at + block] for t in range(middle)], axis=1)
            last = jnp.concatenate([s_ref[t, at : at + block] for t in range(middle, tiles)], axis=1)
            parts.append((near(first + last), near(first - last)))
        for odd in range(2):
            cosine, sine = cos_ref[odd], sin_ref[odd]
            sr, si = parts[0][odd], parts[1][odd]
            factor = green_ref[k : k + block, odd * half : (odd + 1) * half]
            hr = near((dot(sr, cosine) + dot(si, sine)) * factor)
            hi = near((dot(si, cosine) - dot(sr, sine)) * factor)
            back.append((dot_t(cosine, hr) - dot_t(sine, hi), dot_t(cosine, hi) + dot_t(sine, hr)))
        for part, at in enumerate((k, count + k)):
            even, odd = back[0][part], back[1][part]
            lower = near(even + odd)
            p_ref[0:half, at : at + block] = lower
            p_ref[half:nz, at : at + block] = near(even - odd)
            p_ref[nz : nz + 16, at : at + block] = lower[0:16]

    def gather(i, carry):
        c = turn_to(i, 1)
        rec = load(c)
        made = None if wide else tables(rec)
        product(b_ref, (), c, 1, 0, made)
        product(h_ref, (), c, 0, 1, made)
        start = (c * per) // grp * planes
        base = start // fine * fine
        cell = rec[6:7].astype(jnp.int32) + (start - base)
        window = p_ref[pl.ds(pl.multiple_of(base, 16), rows), :]
        level = dot(window, a_ref[c])
        along_x = dot(window, b_ref[...])
        along_y = dot(window, h_ref[...])
        wz = place(spline_weights(rec[3:4]), cell, rows)
        dz = place(spline_slopes(rec[3:4]), cell, rows)

        def total(values):
            return jnp.sum(values, axis=0, keepdims=True)

        terms = jnp.concatenate(
            [total(wz * level), total(wz * along_x), total(wz * along_y), total(dz * level)], axis=0
        )
        for j in range(per):
            at = c * per + j
            terms_ref[at] = terms[:, j * LANE : (j + 1) * LANE]

            @pl.when(at == me)
            def _():
                pltpu.make_async_copy(terms_ref.at[at], held_ref.at[me], got_terms).start()

            @pl.when(at != me)
            def _():
                pltpu.make_async_remote_copy(
                    src_ref=terms_ref.at[at],
                    dst_ref=held_ref.at[me],
                    send_sem=sent_terms,
                    recv_sem=got_terms,
                    device_id=(at % grp, at // grp),
                    device_id_type=pl.DeviceIdType.MESH,
                ).start()

        return carry

    lax.fori_loop(0, chunks, gather, 0)
    all_sent(held_ref, total_slots, got_terms)
    all_sent(held_ref, total_slots - 1, sent_terms)
    all_sent(atoms_ref, total_slots - 1, sent)
    factors = jnp.concatenate([live, loaded, loaded, loaded], axis=0)
    out_ref[...] = jnp.sum(held_ref[...], axis=0) * factors

def digits(value, radix):
    return value // radix, value % radix


def waves_by_parts(weight_sets, cell, first, unit, steps):
    width = cell.shape[1]
    count = steps[0][0].shape[0]
    copies = width // LANE
    low_rows = lax.broadcasted_iota(jnp.int32, (8, width), 0)
    fine_c, fine_s = turn_parts(low_rows.astype(jnp.float32) * unit * cell)
    coarse_rows = (first + 8 * low_rows).astype(jnp.float32) * unit
    coarse_c, coarse_s = turn_parts(coarse_rows * cell)

    def widen(v):
        return jnp.concatenate([v] * copies, axis=1)

    cosines = [widen(c) for c, _ in steps]
    sines = [widen(s) for _, s in steps]
    turned = []
    for i in range(count // 8):
        c, s = coarse_c[i : i + 1], coarse_s[i : i + 1]
        turned.append((c * fine_c - s * fine_s, s * fine_c + c * fine_s))
    cb = jnp.concatenate([c for c, _ in turned], axis=0)
    sb = jnp.concatenate([s for _, s in turned], axis=0)
    out = []
    for w in weight_sets:
        gr = w[0] + sum(w[j + 1] * cosines[j] for j in range(REACH - 1))
        gi = sum(w[j + 1] * sines[j] for j in range(REACH - 1))
        out.append((cb * gr - sb * gi, -(cb * gi + sb * gr)))
    return out


def slab_kernel(
    dims, counts_in, charge_in, frac_in, base_in, green_in, ahead_in, back_in, out_ref,
    counts_ref, charge_ref, frac_ref, base_ref,
    mine_ref, atoms_ref, terms_ref, held_ref, green_ref, turned_ref, ahead_ref, back_ref,
    s_ref, p_ref, x_ref, y_ref, spots_ref, z_ref, hot_ref,
    left_0, left_1, right_0, right_1, sent, got, sent_terms, got_terms, staged
):
    kx, ky, nz, ny, planes, grp, slabs, fine = dims
    group, slab = lax.axis_index("grp"), lax.axis_index("pme")
    me, total_slots, peer = ring_of(slabs, grp)
    wait = meet(total_slots, peer)
    stages = [
        pltpu.make_async_copy(source, target, staged.at[i])
        for i, (source, target) in enumerate(
            [
                (counts_in, counts_ref),
                (charge_in, charge_ref),
                (frac_in, frac_ref),
                (base_in, base_ref),
                (green_in, green_ref),
                (ahead_in, ahead_ref),
                (back_in, back_ref),
            ]
        )
    ]
    for stage in stages:
        stage.start()
    for stage in stages[:4]:
        stage.wait()
    live = live_of(counts_ref, charge_ref.shape)
    loaded = charge_ref[...] * live
    mine_ref[...] = jnp.concatenate(
        [loaded, frac_ref[...], base_ref[...].astype(jnp.float32), live], axis=0
    )
    own = pltpu.make_async_copy(mine_ref, atoms_ref.at[me], got.at[slab])
    own.start()

    wait()

    def send(i, carry):
        pltpu.make_async_remote_copy(
            src_ref=mine_ref,
            dst_ref=atoms_ref.at[me],
            send_sem=sent,
            recv_sem=got.at[slab],
            **peer(i)[1],
        ).start()
        return carry

    lax.fori_loop(1, total_slots, send, 0)

    atoms = charge_ref.shape[1]
    width = grp * atoms
    groups = LANE // ky
    spots = planes // fine
    tiles = spots // groups
    lanes = spots * ky
    reach = fine + REACH - 1
    tall = slabs * fine
    pitch = tall + PAD
    drift = kx + PAD
    quarter = nz // 4
    low_type = jnp.bfloat16
    f32 = jnp.float32
    left_refs, right_refs = (left_0, left_1), (right_0, right_1)
    dot = functools.partial(jnp.dot, preferred_element_type=f32)

    def dot_t(a, b):
        return lax.dot_general(a, b, (((1,), (1,)), ((), ())), preferred_element_type=f32)

    xk = (lax.broadcasted_iota(jnp.int32, (kx, LANE), 0) + group * kx).astype(f32) * (1.0 / NX)
    yk = (lax.broadcasted_iota(jnp.int32, (ky, LANE), 0) + slab * ky).astype(f32) * (1.0 / ny)
    x_steps = [turn_parts(xk * j) for j in range(1, REACH)]
    y_steps = [turn_parts(yk * j) for j in range(1, REACH)]

    for part in range(2):
        for t in range(tiles):
            for z in range(REACH - 1):
                for p in range(slabs):
                    s_ref[part, t, pl.ds(p * fine + z, kx, stride=pitch), :] = jnp.zeros((kx, LANE), f32)
    for stage in stages[4:]:
        stage.wait()
    row = lax.broadcasted_iota(jnp.int32, (nz, nz), 0)
    column = lax.broadcasted_iota(jnp.int32, (nz, nz), 1)
    wanted = 4 * (row % quarter) + row // quarter
    order = jnp.where(column == wanted, 1.0, 0.0).astype(low_type)
    scale = 1.0 / (ny * nz)
    block = 2 * LANE
    for k in range(0, kx * ky, block):
        whole = green_ref[k : k + block] * scale
        high = whole.astype(low_type)
        rest = (whole - high.astype(f32)).astype(low_type)
        turned_ref[:, k : k + block] = dot_t(order, high) + dot_t(order, rest)
    def load(c):
        return jnp.concatenate([atoms_ref[c * grp + i] for i in range(grp)], axis=1)

    def cells(rec):
        cell = rec[6:7].astype(jnp.int32)
        return digits(cell, fine)

    def tile_of(row):
        return jnp.broadcast_to(row, (16, width)).astype(low_type)

    def hot_rows(spot):
        return jnp.where(lax.broadcasted_iota(jnp.int32, (spots, width), 0) == spot, 1.0, 0.0)

    def arrive(i):
        c = slab ^ i
        part = atoms_ref.at[pl.ds(c * grp, grp)]
        pltpu.make_async_copy(part, part, got.at[c]).wait()

    def build(i, side_of):
        c = slab ^ i
        rec = load(c)
        fx, fy, fz = rec[1:2], rec[2:3], rec[3:4]
        wx = [spline_weights(fx), spline_slopes(fx)]
        wy = [[low(w) for w in spline_weights(fy)], [low(w) for w in spline_slopes(fy)]]
        xs = waves_by_parts(wx, rec[4:5], group * kx, 1.0 / NX, x_steps)
        ys = waves_by_parts(wy, rec[5:6], slab * ky, 1.0 / ny, y_steps)
        for kind in range(2):
            for part in range(2):
                x_ref[c, 2 * kind + part] = xs[kind][part]
        for part in range(2):
            y_ref[c, part] = ys[1][part].astype(low_type)
        spot, cell = cells(rec)
        y_low = [ys[0][part].astype(low_type) for part in range(2)]
        hot_ref[side_of] = hot_rows(spot)
        for z in range(spots):
            here = tile_of(hot_ref[side_of, z : z + 1])
            for part in range(2):
                for j in range(0, ky, 16):
                    at = part * lanes + z * ky + j
                    made = y_low[part][j : j + 16] * here
                    spots_ref[c, at : at + 16] = made
                    right_refs[side_of][at : at + 16] = made
        z_ref[side_of] = place(spline_weights(fz), cell, z_ref.shape[1])
        x_low = [(xs[0][part] * rec[0:1]).astype(low_type) for part in range(2)]
        at = 0
        for z in range(reach):
            weight = tile_of(z_ref[side_of, z : z + 1])
            for part in range(2):
                for j in range(0, kx, 16):
                    left_refs[side_of][at : at + 16] = x_low[part][j : j + 16] * weight
                    at += 16

    def mix(i, side_of):
        c = slab ^ i
        made = dot_t(left_refs[side_of][...], right_refs[side_of][...])

        def mesh_rows(z):
            at = 2 * z * kx
            real, imag = made[at : at + kx], made[at + kx : at + 2 * kx]
            return (
                real[:, :lanes] - imag[:, lanes:],
                real[:, lanes:] + imag[:, :lanes],
            )

        following = (c + 1) % slabs
        first = lax.broadcasted_iota(jnp.int32, (kx, lanes), 1) < ky

        def rows_at(slab_of, z):
            return pl.ds(slab_of * fine + z, kx, stride=pitch)

        held = {}
        for z in range(REACH - 1):
            for part in range(2):
                for t in range(tiles):
                    held[z, part, t] = s_ref[part, t, rows_at(c, z), :]
                held[z, part] = s_ref[part, 0, rows_at(following, z), :]
        for z in range(fine):
            values = mesh_rows(z)
            past = mesh_rows(z + fine) if z + fine < reach else None
            for part in range(2):
                value = values[part]
                if past is not None:
                    moved = jnp.concatenate(
                        [past[part][:, lanes - ky :], past[part][:, : lanes - ky]], axis=1
                    )
                    value = value + jnp.where(first, 0.0, moved)
                    s_ref[part, 0, rows_at(following, z), :] = (
                        held[z, part] + jnp.where(first, moved, 0.0)[:, :LANE]
                    )
                for t in range(tiles):
                    out = value[:, t * LANE : (t + 1) * LANE]
                    if past is not None:
                        out = out + held[z, part, t]
                    s_ref[part, t, rows_at(c, z), :] = out

    def two(j, carry):
        arrive(2 * j + 1)
        arrive(2 * j + 2)
        mix(2 * j, 0)
        build(2 * j + 1, 1)
        mix(2 * j + 1, 1)
        build(2 * j + 2, 0)
        return carry

    arrive(0)
    build(0, 0)
    lax.fori_loop(0, slabs // 2 - 1, two, 0)
    arrive(slabs - 1)
    mix(slabs - 2, 0)
    build(slabs - 1, 1)
    mix(slabs - 1, 1)

    side = groups * LANE
    row = lax.broadcasted_iota(jnp.int32, (side, side), 0)
    column = lax.broadcasted_iota(jnp.int32, (side, side), 1)
    wanted = (row % LANE) // ky * LANE + row // LANE * ky + row % ky
    swap = jnp.where(column == wanted, 1.0, 0.0).astype(low_type)
    fewer = slabs // 4
    piece = fewer * fine
    pair = kx // groups

    def near(values):
        return values.astype(low_type)

    def transform(step, carry):
        lefts = []
        for part in range(2):
            for g in range(pair):
                k0 = (step * pair + g) * groups
                for t in range(tiles):
                    lefts.append(
                        jnp.concatenate(
                            [
                                near(s_ref[part, t, pl.ds(pl.multiple_of((k0 + u) * pitch, 8), tall), :])
                                for u in range(groups)
                            ],
                            axis=1,
                        )
                    )
        swapped = dot(jnp.concatenate(lefts, axis=0), swap)
        span = tiles * tall
        picked = []
        for part in range(2):
            halves = [swapped[(part * pair + g) * span : (part * pair + g + 1) * span] for g in range(pair)]
            quarters = []
            for m in range(4):
                blocks = []
                for g in range(groups):
                    for t in range(tiles):
                        at = t * tall + m * piece
                        blocks.append(
                            jnp.concatenate(
                                [half[at : at + piece, g * LANE : (g + 1) * LANE] for half in halves], axis=1
                            )
                        )
                quarters.append(jnp.concatenate(blocks, axis=0))
            picked.append(quarters)
        re, im = picked
        ar, ai, br, bi = re[0] + re[2], im[0] + im[2], re[0] - re[2], im[0] - im[2]
        cr, ci, dr, di = re[1] + re[3], im[1] + im[3], re[1] - re[3], im[1] - im[3]
        mixed = [(ar + cr, ai + ci), (br + di, bi - dr), (ar - cr, ai - ci), (br - di, bi + dr)]
        back = []
        for r in range(4):
            stacked = jnp.concatenate([near(mixed[r][0]), near(mixed[r][1])], axis=0)
            waves = dot(ahead_ref[r], stacked)
            at = pl.ds(pl.multiple_of(step * pair * LANE, LANE), pair * LANE)
            factor = turned_ref[r * quarter : (r + 1) * quarter, at]
            scaled = jnp.concatenate([near(waves[:quarter] * factor), near(waves[quarter:] * factor)], axis=0)
            mesh = dot(back_ref[r], scaled)
            back.append((mesh[:quarter], mesh[quarter:]))
        er, ei = back[0][0] + back[2][0], back[0][1] + back[2][1]
        fr, fi = back[0][0] - back[2][0], back[0][1] - back[2][1]
        ur, ui = back[1][0] + back[3][0], back[1][1] + back[3][1]
        vr, vi = back[1][0] - back[3][0], back[1][1] - back[3][1]
        quarters = [
            (near(er + ur), near(ei + ui)),
            (near(fr - vi), near(fi + vr)),
            (near(er - ur), near(ei - ui)),
            (near(fr + vi), near(fi - vr)),
        ]
        rows = []
        for part in range(2):
            for h in range(pair):
                columns = []
                for g in range(groups):
                    blocks = []
                    for t in range(tiles):
                        for m in range(4):
                            at = (g * tiles + t) * piece
                            blocks.append(quarters[m][part][at : at + piece, h * LANE : (h + 1) * LANE])
                    columns.append(jnp.concatenate(blocks, axis=0))
                rows.append(jnp.concatenate(columns, axis=1))
        spread_out = dot(jnp.concatenate(rows, axis=0), swap)
        for part in range(2):
            for h in range(pair):
                for u in range(groups):
                    k = (step * pair + h) * groups + u
                    for t in range(tiles):
                        at = (part * pair + h) * span + t * tall
                        p_ref[part, t, pl.ds(k, tall, stride=drift), :] = spread_out[
                            at : at + tall, u * LANE : (u + 1) * LANE
                        ]
        return carry

    transform(0, 0)

    def gather(i, carry):
        c = slab ^ (slabs - 1 - i)
        rec = load(c)
        spot, cell = cells(rec)
        z_ref[0] = place(spline_weights(rec[3:4]), cell, z_ref.shape[1])
        z_ref[1] = place(spline_slopes(rec[3:4]), cell, z_ref.shape[1])
        y_low = [y_ref[c, part] for part in range(2)]
        slopes = [[], []]
        hot_ref[0] = hot_rows(spot)
        for z in range(spots):
            here = tile_of(hot_ref[0, z : z + 1])
            for part in range(2):
                slopes[part] += [y_low[part][j : j + 16] * here for j in range(0, ky, 16)]
        slope_spots = jnp.concatenate(slopes[0] + slopes[1], axis=0)
        following = (c + 1) % slabs
        planes_of = []
        for part in range(2):

            def plane(t, slab_of, z):
                return p_ref[part, t, pl.ds(pl.multiple_of((slab_of * fine + z) * drift, 8), kx), :]

            mains = [jnp.concatenate([plane(t, c, z) for t in range(tiles)], axis=1) for z in range(fine)]
            extras = [
                jnp.concatenate([mains[z][:, ky:], plane(0, following, z)[:, :ky]], axis=1)
                for z in range(REACH - 1)
            ]
            planes_of.append(near(jnp.concatenate(mains + extras, axis=0)))
        lefts = (
            jnp.concatenate([planes_of[0], planes_of[1]], axis=1),
            jnp.concatenate([planes_of[1], -planes_of[0]], axis=1),
        )
        totals = [jnp.zeros((kx, width), f32)] * 4
        for part in range(2):
            level = dot(lefts[part], spots_ref[c])
            slope = dot(lefts[part], slope_spots)
            q = qd = qz = None
            for z in range(reach):
                w = z_ref[0, z : z + 1]
                d = z_ref[1, z : z + 1]
                here = level[z * kx : (z + 1) * kx]
                there = slope[z * kx : (z + 1) * kx]
                q = here * w if q is None else q + here * w
                qz = here * d if qz is None else qz + here * d
                qd = there * w if qd is None else qd + there * w
            x, dx = x_ref[c, part], x_ref[c, 2 + part]
            totals = [totals[0] + x * q, totals[1] + dx * q, totals[2] + x * qd, totals[3] + x * qz]
        terms = jnp.concatenate([jnp.sum(t, axis=0, keepdims=True) for t in totals], axis=0)
        for j in range(grp):
            at = c * grp + j
            terms_ref[at] = terms[:, j * atoms : (j + 1) * atoms]

            @pl.when(at == me)
            def _():
                pltpu.make_async_copy(terms_ref.at[at], held_ref.at[me], got_terms).start()

            @pl.when(at != me)
            def _():
                pltpu.make_async_remote_copy(
                    src_ref=terms_ref.at[at],
                    dst_ref=held_ref.at[me],
                    send_sem=sent_terms,
                    recv_sem=got_terms,
                    device_id=(j, c),
                    device_id_type=pl.DeviceIdType.MESH,
                ).start()

        return carry

    lax.fori_loop(0, slabs, gather, 0)
    all_sent(held_ref, total_slots, got_terms)
    all_sent(held_ref, total_slots - 1, sent_terms)
    all_sent(atoms_ref, total_slots - 1, sent)
    factors = jnp.concatenate([live, loaded, loaded, loaded], axis=0)
    out_ref[...] = jnp.sum(held_ref[...], axis=0) * factors


def ring_of(slabs, groups):
    total = slabs * groups
    me = lax.axis_index("pme") * groups + lax.axis_index("grp")

    def peer(i):
        at = me ^ i if total & (total - 1) == 0 else (me + i) % total
        return at, {
            "device_id": (at % groups, at // groups),
            "device_id_type": pl.DeviceIdType.MESH,
        }

    return me, total, peer


def meet(total, peer):
    barrier = pltpu.get_barrier_semaphore()

    def signal(i, carry):
        pl.semaphore_signal(barrier, inc=1, **peer(i)[1])
        return carry

    lax.fori_loop(1, total, signal, 0)
    return lambda: pl.semaphore_wait(barrier, total - 1)


def all_sent(ref, total, sem):
    part = ref.at[pl.ds(0, total)]
    pltpu.make_async_copy(part, part, sem).wait()


def live_of(counts_ref, shape):
    return jnp.where(lax.broadcasted_iota(jnp.int32, shape, 1) < counts_ref[0], 1.0, 0.0)


def body(slabs, groups, charge, base, frac, counts, green):
    atoms = charge.shape[0]
    kx, ky, nz = green.shape
    ny = ky * slabs
    planes = nz // slabs
    if fits(kx, ky, planes, slabs, atoms, FINE):
        return slab_body(slabs, groups, FINE, charge, base, frac, counts, green)
    slots = slabs * groups
    per = math.gcd(groups, 4)
    chunks = slots // per
    smem = pl.BlockSpec(memory_space=pltpu.SMEM)
    vmem = pl.BlockSpec(memory_space=VMEM)
    free = pl.BlockSpec(memory_space=pl.ANY)
    dma = pltpu.SemaphoreType.DMA
    index = np.arange(nz // 2)
    waves = np.stack([2 * index, 2 * index + 1])
    angle = (index[None, :, None] * waves[:, None, :] % nz) * (2.0 * math.pi / nz)
    cosine = np.cos(angle).astype(ml_dtypes.bfloat16)
    sine = np.sin(angle).astype(ml_dtypes.bfloat16)
    count = kx * ky
    width = per * atoms
    low_type = jnp.bfloat16
    wide = ky % 16 == 0
    return pl.pallas_call(
        functools.partial(mesh_kernel, (kx, ky, nz, ny, planes, groups, per, chunks, slabs)),
        out_shape=jax.ShapeDtypeStruct((4, atoms), jnp.float32),
        in_specs=[smem] + [vmem] * 3 + [free] * 3,
        out_specs=vmem,
        scratch_shapes=[
            VMEM((8, atoms), jnp.float32),
            VMEM((slots, 8, atoms), jnp.float32),
            VMEM((slots, 4, atoms), jnp.float32),
            VMEM((slots, 4, atoms), jnp.float32),
            VMEM((count, nz), jnp.float32),
            VMEM((2, nz // 2, nz // 2), low_type),
            VMEM((2, nz // 2, nz // 2), low_type),
            VMEM((chunks, 2 * count, width), low_type),
            VMEM((2 * count, width), low_type),
            VMEM((nz // LANE, 2 * count, LANE), jnp.float32),
            VMEM((2 * count, width), low_type),
            VMEM((nz + 16, 2 * count), low_type),
            VMEM((chunks, 4, kx, width) if wide else (1, 4, 8, LANE), jnp.float32),
            VMEM((chunks, 4, ky, width) if wide else (1, 4, 8, LANE), low_type),
            dma,
            dma((slabs,)),
            dma,
            dma,
            dma((3,)),
        ],
        compiler_params=pltpu.CompilerParams(
            collective_id=1, has_side_effects=True, vmem_limit_bytes=60 * 1024 * 1024
        ),
    )(counts, charge.reshape(1, atoms), frac, base, green.reshape(count, nz), cosine, sine)

def turns_of(nz, planes, fine, groups, tiles, fewer):
    quarter = nz // 4
    g, t, p, z = np.meshgrid(
        np.arange(groups), np.arange(tiles), np.arange(fewer), np.arange(fine), indexing="ij"
    )
    place_of = (p * planes + (t * groups + g) * fine + z).reshape(-1)
    ahead = []
    for r in range(4):
        wave = 4 * np.arange(quarter) + r
        angle = (wave[:, None] * place_of[None, :] % nz) * (2.0 * math.pi / nz)
        cosine, sine = np.cos(angle), np.sin(angle)
        ahead.append(np.block([[cosine, sine], [-sine, cosine]]))
    ahead = np.stack(ahead)
    return ahead.astype(ml_dtypes.bfloat16), ahead.transpose(0, 2, 1).astype(ml_dtypes.bfloat16)


def fits(kx, ky, planes, slabs, atoms, fine):
    if ky % 16 or LANE % ky or kx % 16 or slabs % 4 or planes % fine or atoms % LANE:
        return False
    if slabs & (slabs - 1) or kx > 64 or ky > 64:
        return False
    groups = LANE // ky
    return (
        (planes // fine) % groups == 0
        and kx % groups == 0
        and (slabs // 4 * fine) % 16 == 0
        and fine % 8 == 0
        and fine + REACH - 1 <= 24
    )


def slab_body(slabs, groups, fine, charge, base, frac, counts, green):
    atoms = charge.shape[0]
    kx, ky, nz = green.shape
    ny = ky * slabs
    planes = nz // slabs
    slots = slabs * groups
    width = groups * atoms
    count = kx * ky
    spots = planes // fine
    sets = LANE // ky
    tiles = spots // sets
    ahead, back = turns_of(nz, planes, fine, sets, tiles, slabs // 4)
    vmem = pl.BlockSpec(memory_space=VMEM)
    free = pl.BlockSpec(memory_space=pl.ANY)
    dma = pltpu.SemaphoreType.DMA
    low_type = jnp.bfloat16
    f32 = jnp.float32
    tall = slabs * fine
    reach = fine + REACH - 1
    return pl.pallas_call(
        functools.partial(slab_kernel, (kx, ky, nz, ny, planes, groups, slabs, fine)),
        out_shape=jax.ShapeDtypeStruct((4, atoms), f32),
        in_specs=[free] * 7,
        out_specs=vmem,
        scratch_shapes=[
            pltpu.SMEM((1,), jnp.int32),
            VMEM((1, atoms), f32),
            VMEM((3, atoms), f32),
            VMEM((3, atoms), jnp.int32),
            VMEM((8, atoms), f32),
            VMEM((slots, 8, atoms), f32),
            VMEM((slots, 4, atoms), f32),
            VMEM((slots, 4, atoms), f32),
            VMEM((count, nz), f32),
            VMEM((nz, count), f32),
            VMEM(ahead.shape, low_type),
            VMEM(back.shape, low_type),
            VMEM((2, tiles, kx * (tall + PAD), LANE), f32),
            VMEM((2, tiles, tall * (kx + PAD), LANE), f32),
            VMEM((slabs, 4, kx, width), f32),
            VMEM((slabs, 2, ky, width), low_type),
            VMEM((slabs, 2 * spots * ky, width), low_type),
            VMEM((2, 24, width), f32),
            VMEM((2, spots, width), f32),
            VMEM((2 * reach * kx, width), low_type),
            VMEM((2 * reach * kx, width), low_type),
            VMEM((2 * spots * ky, width), low_type),
            VMEM((2 * spots * ky, width), low_type),
            dma,
            dma((slabs,)),
            dma,
            dma,
            dma((7,)),
        ],
        compiler_params=pltpu.CompilerParams(
            collective_id=2, has_side_effects=True, vmem_limit_bytes=60 * 1024 * 1024
        ),
    )(counts, charge.reshape(1, atoms), frac, base, green.reshape(count, nz), ahead, back)


def solution(mesh):
    placed = (
        P(("grp", "pme")),
        P(None, ("grp", "pme")),
        P(None, ("grp", "pme")),
        P(("grp", "pme")),
        P("grp", "pme", None),
    )
    return jax.shard_map(
        functools.partial(body, mesh.shape["pme"], mesh.shape["grp"]),
        mesh=mesh,
        in_specs=placed,
        out_specs=P(None, ("grp", "pme")),
        check_vma=False,
    )
```

```python
import functools
import math

import jax
import jax.numpy as jnp
import ml_dtypes
import numpy as np
from jax import lax
from jax.experimental import pallas as pl
from jax.experimental.pallas import tpu as pltpu
from jax.sharding import PartitionSpec as P

NX = 256
LANE = 128
REACH = 4
FINE = 16
PAD = 8
VMEM = pltpu.VMEM


def spline_weights(u):
    v = 1.0 - u
    u2 = u * u
    u3 = u2 * u
    return (
        v * v * v / 6.0,
        (3.0 * u3 - 6.0 * u2 + 4.0) / 6.0,
        (-3.0 * u3 + 3.0 * u2 + 3.0 * u + 1.0) / 6.0,
        u3 / 6.0,
    )


def spline_slopes(u):
    v = 1.0 - u
    u2 = u * u
    return (
        -v * v / 2.0,
        (3.0 * u2 - 4.0 * u) / 2.0,
        (-3.0 * u2 + 2.0 * u + 1.0) / 2.0,
        u2 / 2.0,
    )


def turn_parts(turns):
    x = (turns - jnp.floor(turns + 0.5)) * math.pi
    y = x * x
    s = 1.0 / 362880.0 - y * (1.0 / 39916800.0)
    s = -1.0 / 5040.0 + y * s
    s = 1.0 / 120.0 + y * s
    s = -1.0 / 6.0 + y * s
    s = x + x * (y * s)
    c = -1.0 / 3628800.0 + y * (1.0 / 479001600.0)
    c = 1.0 / 40320.0 + y * c
    c = -1.0 / 720.0 + y * c
    c = 1.0 / 24.0 + y * c
    c = -0.5 + y * c
    c = 1.0 + y * c
    return (1.0 - 2.0 * s * s, 2.0 * s * c)


def waves_of(weight_sets, cell, waves, steps):
    copies = cell.shape[1] // waves.shape[1]

    def widen(v):
        return jnp.concatenate([v] * copies, axis=1)

    cb, sb = turn_parts(widen(waves) * cell)
    cosines = [widen(c) for c, _ in steps]
    sines = [widen(s) for _, s in steps]
    out = []
    for w in weight_sets:
        gr = w[0] + sum(w[j + 1] * cosines[j] for j in range(REACH - 1))
        gi = sum(w[j + 1] * sines[j] for j in range(REACH - 1))
        out.append((cb * gr - sb * gi, -(cb * gi + sb * gr)))
    return out


def low(values):
    return values.astype(jnp.bfloat16).astype(jnp.float32)


def place(weights, cell, rows):
    z = lax.broadcasted_iota(jnp.int32, (rows, cell.shape[1]), 0) - cell
    total = jnp.where(z == 0, weights[0], 0.0)
    for j in range(1, REACH):
        total = jnp.where(z == j, weights[j], total)
    return total


def mesh_kernel(
    dims, counts_ref, charge_ref, frac_ref, base_ref, green_in, cos_in, sin_in, out_ref,
    mine_ref, atoms_ref, terms_ref, held_ref, green_ref, cos_ref, sin_ref,
    a_ref, b_ref, s_ref, h_ref, p_ref, x_ref, y_ref, sent, got, sent_terms, got_terms, staged
):
    kx, ky, nz, ny, planes, grp, per, chunks, slabs = dims
    group, slab = lax.axis_index("grp"), lax.axis_index("pme")
    me, total_slots, peer = ring_of(slabs, grp)
    wait = meet(total_slots, peer)
    stages = [
        pltpu.make_async_copy(source, target, staged.at[i])
        for i, (source, target) in enumerate(
            [(green_in, green_ref), (cos_in, cos_ref), (sin_in, sin_ref)]
        )
    ]
    for stage in stages:
        stage.start()
    live = live_of(counts_ref, charge_ref.shape)
    loaded = charge_ref[...] * live
    mine_ref[...] = jnp.concatenate(
        [loaded, frac_ref[...], base_ref[...].astype(jnp.float32), live], axis=0
    )
    own = pltpu.make_async_copy(mine_ref, atoms_ref.at[me], got.at[slab])
    own.start()
    count = kx * ky
    width = per * LANE
    tiles = nz // LANE
    fine = min(64, LANE)
    rows = fine + 16
    wide = ky % 16 == 0

    if wide:
        xk = lax.broadcasted_iota(jnp.int32, (kx, LANE), 0)
        yk = lax.broadcasted_iota(jnp.int32, (ky, LANE), 0)
    else:
        index = lax.broadcasted_iota(jnp.int32, (count, LANE), 0)
        xk, yk = index // ky, index % ky
    xk = (xk + group * kx).astype(jnp.float32) * (1.0 / NX)
    yk = (yk + slab * ky).astype(jnp.float32) * (1.0 / ny)
    x_steps = [turn_parts(xk * j) for j in range(1, REACH)]
    y_steps = [turn_parts(yk * j) for j in range(1, REACH)]

    s_ref[...] = jnp.zeros_like(s_ref)
    dot = functools.partial(jnp.dot, preferred_element_type=jnp.float32)
    half = nz // 2
    scale = 1.0 / (ny * nz)
    for stage in stages:
        stage.wait()
    lane_in = lax.broadcasted_iota(jnp.int32, (nz, nz), 0)
    lane_out = lax.broadcasted_iota(jnp.int32, (nz, nz), 1)
    wanted = jnp.where(lane_out < half, 2 * lane_out, 2 * (lane_out - half) + 1)
    order = jnp.where(lane_in == wanted, 1.0, 0.0).astype(jnp.bfloat16)
    block = min(256, count)
    for k in range(0, count, block):
        whole = green_ref[k : k + block] * scale
        high = whole.astype(jnp.bfloat16)
        rest = (whole - high.astype(jnp.float32)).astype(jnp.bfloat16)
        green_ref[k : k + block] = dot(high, order) + dot(rest, order)
    wait()

    def send(i, carry):
        pltpu.make_async_remote_copy(
            src_ref=mine_ref,
            dst_ref=atoms_ref.at[me],
            send_sem=sent,
            recv_sem=got.at[slab],
            **peer(i)[1],
        ).start()
        return carry

    lax.fori_loop(1, total_slots, send, 0)
    share = grp // per

    def turn_to(i, ahead):
        return (slab + ahead + i // share) % slabs * share + i % share

    def load(c):
        return jnp.concatenate([atoms_ref[c * per + i] for i in range(per)], axis=1)

    def tables(rec):
        fx, fy = rec[1:2], rec[2:3]
        wx = [spline_weights(fx), spline_slopes(fx)]
        wy = [[low(w) for w in spline_weights(fy)], [low(w) for w in spline_slopes(fy)]]
        return waves_of(wx, rec[4:5], xk, x_steps), waves_of(wy, rec[5:6], yk, y_steps)

    def keep(c, rec):
        for kind, (x, y) in enumerate(zip(*tables(rec))):
            for part in range(2):
                x_ref[c, 2 * kind + part] = x[part]
                y_ref[c, 2 * kind + part] = y[part].astype(jnp.bfloat16)

    def row_of(c, kind, i):
        return [
            jnp.broadcast_to(x_ref[c, 2 * kind + part, i : i + 1], (16, width)).astype(jnp.bfloat16)
            for part in range(2)
        ]

    def product(ref, lead, c, x_kind, y_kind, made):
        if not wide:
            (xr, xi), (yr, yi) = made[0][x_kind], made[1][y_kind]
            ref[lead + (slice(0, count),)] = (xr * yr - xi * yi).astype(jnp.bfloat16)
            ref[lead + (slice(count, 2 * count),)] = (xr * yi + xi * yr).astype(jnp.bfloat16)
            return
        for i in range(kx):
            row = row_of(c, x_kind, i)
            for j in range(0, ky, 16):
                yr = y_ref[c, 2 * y_kind, j : j + 16]
                yi = y_ref[c, 2 * y_kind + 1, j : j + 16]
                at = i * ky + j
                ref[lead + (slice(at, at + 16),)] = row[0] * yr - row[1] * yi
                ref[lead + (slice(count + at, count + at + 16),)] = row[0] * yi + row[1] * yr

    def arrive(i):
        c = turn_to(i, 0)

        @pl.when(i % share == 0)
        def _():
            part = atoms_ref.at[pl.ds(c * per, grp)]
            pltpu.make_async_copy(part, part, got.at[c // share]).wait()

        return c

    def spread(i, carry):
        c = arrive(i)
        rec = load(c)
        start = (c * per) // grp * planes
        tile = start // LANE
        cell = rec[6:7].astype(jnp.int32) + (start - tile * LANE)
        wz = [rec[0:1] * w for w in spline_weights(rec[3:4])]
        table = place(wz, cell, LANE + 16).astype(jnp.bfloat16)
        rest = jnp.zeros((LANE - 16, width), jnp.bfloat16)
        table = jnp.concatenate([table, rest], axis=0)
        following = lax.rem(tile + 1, tiles)

        def add(at, size, block):
            part = lax.dot_general(
                block, table, (((1,), (1,)), ((), ())), preferred_element_type=jnp.float32
            )
            s_ref[tile, at : at + size] += part[:, :LANE]
            s_ref[following, at : at + size] += part[:, LANE:]

        if not wide:
            product(a_ref, (c,), c, 0, 0, tables(rec))
            add(0, 2 * count, a_ref[c])
            return carry
        keep(c, rec)
        some = max(1, 256 // ky)
        for i0 in range(0, kx, some):
            blocks = ([], [])
            for k in range(i0, min(i0 + some, kx)):
                row = row_of(c, 0, k)
                for j in range(0, ky, 16):
                    yr, yi = y_ref[c, 0, j : j + 16], y_ref[c, 1, j : j + 16]
                    blocks[0].append(row[0] * yr - row[1] * yi)
                    blocks[1].append(row[0] * yi + row[1] * yr)
            for part in range(2):
                block = jnp.concatenate(blocks[part], axis=0)
                at, size = part * count + i0 * ky, block.shape[0]
                a_ref[c, at : at + size] = block
                add(at, size, block)
        return carry

    lax.fori_loop(0, chunks, spread, 0)

    def dot_t(a, b):
        return lax.dot_general(a, b, (((1,), (1,)), ((), ())), preferred_element_type=jnp.float32)

    def near(values):
        return values.astype(jnp.bfloat16)

    middle = tiles // 2
    for k in range(0, count, block):
        back = []
        parts = []
        for at in (k, count + k):
            first = jnp.concatenate([s_ref[t, at : at + block] for t in range(middle)], axis=1)
            last = jnp.concatenate([s_ref[t, at : at + block] for t in range(middle, tiles)], axis=1)
            parts.append((near(first + last), near(first - last)))
        for odd in range(2):
            cosine, sine = cos_ref[odd], sin_ref[odd]
            sr, si = parts[0][odd], parts[1][odd]
            factor = green_ref[k : k + block, odd * half : (odd + 1) * half]
            hr = near((dot(sr, cosine) + dot(si, sine)) * factor)
            hi = near((dot(si, cosine) - dot(sr, sine)) * factor)
            back.append((dot_t(cosine, hr) - dot_t(sine, hi), dot_t(cosine, hi) + dot_t(sine, hr)))
        for part, at in enumerate((k, count + k)):
            even, odd = back[0][part], back[1][part]
            lower = near(even + odd)
            p_ref[0:half, at : at + block] = lower
            p_ref[half:nz, at : at + block] = near(even - odd)
            p_ref[nz : nz + 16, at : at + block] = lower[0:16]

    def gather(i, carry):
        c = turn_to(i, 1)
        rec = load(c)
        made = None if wide else tables(rec)
        product(b_ref, (), c, 1, 0, made)
        product(h_ref, (), c, 0, 1, made)
        start = (c * per) // grp * planes
        base = start // fine * fine
        cell = rec[6:7].astype(jnp.int32) + (start - base)
        window = p_ref[pl.ds(pl.multiple_of(base, 16), rows), :]
        level = dot(window, a_ref[c])
        along_x = dot(window, b_ref[...])
        along_y = dot(window, h_ref[...])
        wz = place(spline_weights(rec[3:4]), cell, rows)
        dz = place(spline_slopes(rec[3:4]), cell, rows)

        def total(values):
            return jnp.sum(values, axis=0, keepdims=True)

        terms = jnp.concatenate(
            [total(wz * level), total(wz * along_x), total(wz * along_y), total(dz * level)], axis=0
        )
        for j in range(per):
            at = c * per + j
            terms_ref[at] = terms[:, j * LANE : (j + 1) * LANE]

            @pl.when(at == me)
            def _():
                pltpu.make_async_copy(terms_ref.at[at], held_ref.at[me], got_terms).start()

            @pl.when(at != me)
            def _():
                pltpu.make_async_remote_copy(
                    src_ref=terms_ref.at[at],
                    dst_ref=held_ref.at[me],
                    send_sem=sent_terms,
                    recv_sem=got_terms,
                    device_id=(at % grp, at // grp),
                    device_id_type=pl.DeviceIdType.MESH,
                ).start()

        return carry

    lax.fori_loop(0, chunks, gather, 0)
    all_sent(held_ref, total_slots, got_terms)
    all_sent(held_ref, total_slots - 1, sent_terms)
    all_sent(atoms_ref, total_slots - 1, sent)
    factors = jnp.concatenate([live, loaded, loaded, loaded], axis=0)
    out_ref[...] = jnp.sum(held_ref[...], axis=0) * factors

def digits(value, radix):
    return value // radix, value % radix


def waves_by_parts(weight_sets, cell, first, unit, steps):
    width = cell.shape[1]
    count = steps[0][0].shape[0]
    copies = width // LANE
    low_rows = lax.broadcasted_iota(jnp.int32, (8, width), 0)
    fine_c, fine_s = turn_parts(low_rows.astype(jnp.float32) * unit * cell)
    coarse_rows = (first + 8 * low_rows).astype(jnp.float32) * unit
    coarse_c, coarse_s = turn_parts(coarse_rows * cell)

    def widen(v):
        return jnp.concatenate([v] * copies, axis=1)

    cosines = [widen(c) for c, _ in steps]
    sines = [widen(s) for _, s in steps]
    turned = []
    for i in range(count // 8):
        c, s = coarse_c[i : i + 1], coarse_s[i : i + 1]
        turned.append((c * fine_c - s * fine_s, s * fine_c + c * fine_s))
    cb = jnp.concatenate([c for c, _ in turned], axis=0)
    sb = jnp.concatenate([s for _, s in turned], axis=0)
    out = []
    for w in weight_sets:
        gr = w[0] + sum(w[j + 1] * cosines[j] for j in range(REACH - 1))
        gi = sum(w[j + 1] * sines[j] for j in range(REACH - 1))
        out.append((cb * gr - sb * gi, -(cb * gi + sb * gr)))
    return out


def slab_kernel(
    dims, counts_in, charge_in, frac_in, base_in, green_in, ahead_in, back_in, out_ref,
    counts_ref, charge_ref, frac_ref, base_ref,
    mine_ref, atoms_ref, terms_ref, held_ref, green_ref, turned_ref, ahead_ref, back_ref,
    s_ref, p_ref, x_ref, y_ref, spots_ref, z_ref, hot_ref,
    left_0, left_1, right_0, right_1, sent, got, sent_terms, got_terms, staged
):
    kx, ky, nz, ny, planes, grp, slabs, fine = dims
    group, slab = lax.axis_index("grp"), lax.axis_index("pme")
    me, total_slots, peer = ring_of(slabs, grp)
    wait = meet(total_slots, peer)
    stages = [
        pltpu.make_async_copy(source, target, staged.at[i])
        for i, (source, target) in enumerate(
            [
                (counts_in, counts_ref),
                (charge_in, charge_ref),
                (frac_in, frac_ref),
                (base_in, base_ref),
                (green_in, green_ref),
                (ahead_in, ahead_ref),
                (back_in, back_ref),
            ]
        )
    ]
    for stage in stages:
        stage.start()
    for stage in stages[:4]:
        stage.wait()
    live = live_of(counts_ref, charge_ref.shape)
    loaded = charge_ref[...] * live
    mine_ref[...] = jnp.concatenate(
        [loaded, frac_ref[...], base_ref[...].astype(jnp.float32), live], axis=0
    )
    own = pltpu.make_async_copy(mine_ref, atoms_ref.at[me], got.at[slab])
    own.start()

    wait()

    def send(i, carry):
        pltpu.make_async_remote_copy(
            src_ref=mine_ref,
            dst_ref=atoms_ref.at[me],
            send_sem=sent,
            recv_sem=got.at[slab],
            **peer(i)[1],
        ).start()
        return carry

    lax.fori_loop(1, total_slots, send, 0)

    atoms = charge_ref.shape[1]
    width = grp * atoms
    groups = LANE // ky
    spots = planes // fine
    tiles = spots // groups
    lanes = spots * ky
    reach = fine + REACH - 1
    tall = slabs * fine
    pitch = tall + PAD
    drift = kx + PAD
    quarter = nz // 4
    low_type = jnp.bfloat16
    f32 = jnp.float32
    left_refs, right_refs = (left_0, left_1), (right_0, right_1)
    dot = functools.partial(jnp.dot, preferred_element_type=f32)

    def dot_t(a, b):
        return lax.dot_general(a, b, (((1,), (1,)), ((), ())), preferred_element_type=f32)

    xk = (lax.broadcasted_iota(jnp.int32, (kx, LANE), 0) + group * kx).astype(f32) * (1.0 / NX)
    yk = (lax.broadcasted_iota(jnp.int32, (ky, LANE), 0) + slab * ky).astype(f32) * (1.0 / ny)
    x_steps = [turn_parts(xk * j) for j in range(1, REACH)]
    y_steps = [turn_parts(yk * j) for j in range(1, REACH)]

    for part in range(2):
        for t in range(tiles):
            for z in range(REACH - 1):
                for p in range(slabs):
                    s_ref[part, t, pl.ds(p * fine + z, kx, stride=pitch), :] = jnp.zeros((kx, LANE), f32)
    for stage in stages[4:]:
        stage.wait()
    row = lax.broadcasted_iota(jnp.int32, (nz, nz), 0)
    column = lax.broadcasted_iota(jnp.int32, (nz, nz), 1)
    wanted = 4 * (row % quarter) + row // quarter
    order = jnp.where(column == wanted, 1.0, 0.0).astype(low_type)
    scale = 1.0 / (ny * nz)
    block = 2 * LANE
    for k in range(0, kx * ky, block):
        whole = green_ref[k : k + block] * scale
        high = whole.astype(low_type)
        rest = (whole - high.astype(f32)).astype(low_type)
        turned_ref[:, k : k + block] = dot_t(order, high) + dot_t(order, rest)
    def load(c):
        return jnp.concatenate([atoms_ref[c * grp + i] for i in range(grp)], axis=1)

    def cells(rec):
        cell = rec[6:7].astype(jnp.int32)
        return digits(cell, fine)

    def tile_of(row):
        return jnp.broadcast_to(row, (16, width)).astype(low_type)

    def hot_rows(spot):
        return jnp.where(lax.broadcasted_iota(jnp.int32, (spots, width), 0) == spot, 1.0, 0.0)

    def arrive(i):
        c = slab ^ i
        part = atoms_ref.at[pl.ds(c * grp, grp)]
        pltpu.make_async_copy(part, part, got.at[c]).wait()

    def build(i, side_of):
        c = slab ^ i
        rec = load(c)
        fx, fy, fz = rec[1:2], rec[2:3], rec[3:4]
        wx = [spline_weights(fx), spline_slopes(fx)]
        wy = [[low(w) for w in spline_weights(fy)], [low(w) for w in spline_slopes(fy)]]
        xs = waves_by_parts(wx, rec[4:5], group * kx, 1.0 / NX, x_steps)
        ys = waves_by_parts(wy, rec[5:6], slab * ky, 1.0 / ny, y_steps)
        for kind in range(2):
            for part in range(2):
                x_ref[c, 2 * kind + part] = xs[kind][part]
        for part in range(2):
            y_ref[c, part] = ys[1][part].astype(low_type)
        spot, cell = cells(rec)
        y_low = [ys[0][part].astype(low_type) for part in range(2)]
        hot_ref[side_of] = hot_rows(spot)
        for z in range(spots):
            here = tile_of(hot_ref[side_of, z : z + 1])
            for part in range(2):
                for j in range(0, ky, 16):
                    at = part * lanes + z * ky + j
                    made = y_low[part][j : j + 16] * here
                    spots_ref[c, at : at + 16] = made
                    right_refs[side_of][at : at + 16] = made
        z_ref[side_of] = place(spline_weights(fz), cell, z_ref.shape[1])
        x_low = [(xs[0][part] * rec[0:1]).astype(low_type) for part in range(2)]
        at = 0
        for z in range(reach):
            weight = tile_of(z_ref[side_of, z : z + 1])
            for part in range(2):
                for j in range(0, kx, 16):
                    left_refs[side_of][at : at + 16] = x_low[part][j : j + 16] * weight
                    at += 16

    def mix(i, side_of):
        c = slab ^ i
        made = dot_t(left_refs[side_of][...], right_refs[side_of][...])

        def mesh_rows(z):
            at = 2 * z * kx
            real, imag = made[at : at + kx], made[at + kx : at + 2 * kx]
            return (
                real[:, :lanes] - imag[:, lanes:],
                real[:, lanes:] + imag[:, :lanes],
            )

        following = (c + 1) % slabs
        first = lax.broadcasted_iota(jnp.int32, (kx, lanes), 1) < ky

        def rows_at(slab_of, z):
            return pl.ds(slab_of * fine + z, kx, stride=pitch)

        held = {}
        for z in range(REACH - 1):
            for part in range(2):
                for t in range(tiles):
                    held[z, part, t] = s_ref[part, t, rows_at(c, z), :]
                held[z, part] = s_ref[part, 0, rows_at(following, z), :]
        for z in range(fine):
            values = mesh_rows(z)
            past = mesh_rows(z + fine) if z + fine < reach else None
            for part in range(2):
                value = values[part]
                if past is not None:
                    moved = jnp.concatenate(
                        [past[part][:, lanes - ky :], past[part][:, : lanes - ky]], axis=1
                    )
                    value = value + jnp.where(first, 0.0, moved)
                    s_ref[part, 0, rows_at(following, z), :] = (
                        held[z, part] + jnp.where(first, moved, 0.0)[:, :LANE]
                    )
                for t in range(tiles):
                    out = value[:, t * LANE : (t + 1) * LANE]
                    if past is not None:
                        out = out + held[z, part, t]
                    s_ref[part, t, rows_at(c, z), :] = out

    def two(j, carry):
        arrive(2 * j + 1)
        arrive(2 * j + 2)
        mix(2 * j, 0)
        build(2 * j + 1, 1)
        mix(2 * j + 1, 1)
        build(2 * j + 2, 0)
        return carry

    arrive(0)
    build(0, 0)
    lax.fori_loop(0, slabs // 2 - 1, two, 0)
    arrive(slabs - 1)
    mix(slabs - 2, 0)
    build(slabs - 1, 1)
    mix(slabs - 1, 1)

    side = groups * LANE
    row = lax.broadcasted_iota(jnp.int32, (side, side), 0)
    column = lax.broadcasted_iota(jnp.int32, (side, side), 1)
    wanted = (row % LANE) // ky * LANE + row // LANE * ky + row % ky
    swap = jnp.where(column == wanted, 1.0, 0.0).astype(low_type)
    fewer = slabs // 4
    piece = fewer * fine
    pair = kx // groups

    def near(values):
        return values.astype(low_type)

    def transform(step, carry):
        lefts = []
        for part in range(2):
            for g in range(pair):
                k0 = (step * pair + g) * groups
                for t in range(tiles):
                    lefts.append(
                        jnp.concatenate(
                            [
                                near(s_ref[part, t, pl.ds(pl.multiple_of((k0 + u) * pitch, 8), tall), :])
                                for u in range(groups)
                            ],
                            axis=1,
                        )
                    )
        swapped = dot(jnp.concatenate(lefts, axis=0), swap)
        span = tiles * tall
        picked = []
        for part in range(2):
            halves = [swapped[(part * pair + g) * span : (part * pair + g + 1) * span] for g in range(pair)]
            quarters = []
            for m in range(4):
                blocks = []
                for g in range(groups):
                    for t in range(tiles):
                        at = t * tall + m * piece
                        blocks.append(
                            jnp.concatenate(
                                [half[at : at + piece, g * LANE : (g + 1) * LANE] for half in halves], axis=1
                            )
                        )
                quarters.append(jnp.concatenate(blocks, axis=0))
            picked.append(quarters)
        re, im = picked
        ar, ai, br, bi = re[0] + re[2], im[0] + im[2], re[0] - re[2], im[0] - im[2]
        cr, ci, dr, di = re[1] + re[3], im[1] + im[3], re[1] - re[3], im[1] - im[3]
        mixed = [(ar + cr, ai + ci), (br + di, bi - dr), (ar - cr, ai - ci), (br - di, bi + dr)]
        back = []
        for r in range(4):
            stacked = jnp.concatenate([near(mixed[r][0]), near(mixed[r][1])], axis=0)
            waves = dot(ahead_ref[r], stacked)
            at = pl.ds(pl.multiple_of(step * pair * LANE, LANE), pair * LANE)
            factor = turned_ref[r * quarter : (r + 1) * quarter, at]
            scaled = jnp.concatenate([near(waves[:quarter] * factor), near(waves[quarter:] * factor)], axis=0)
            mesh = dot(back_ref[r], scaled)
            back.append((mesh[:quarter], mesh[quarter:]))
        er, ei = back[0][0] + back[2][0], back[0][1] + back[2][1]
        fr, fi = back[0][0] - back[2][0], back[0][1] - back[2][1]
        ur, ui = back[1][0] + back[3][0], back[1][1] + back[3][1]
        vr, vi = back[1][0] - back[3][0], back[1][1] - back[3][1]
        quarters = [
            (near(er + ur), near(ei + ui)),
            (near(fr - vi), near(fi + vr)),
            (near(er - ur), near(ei - ui)),
            (near(fr + vi), near(fi - vr)),
        ]
        rows = []
        for part in range(2):
            for h in range(pair):
                columns = []
                for g in range(groups):
                    blocks = []
                    for t in range(tiles):
                        for m in range(4):
                            at = (g * tiles + t) * piece
                            blocks.append(quarters[m][part][at : at + piece, h * LANE : (h + 1) * LANE])
                    columns.append(jnp.concatenate(blocks, axis=0))
                rows.append(jnp.concatenate(columns, axis=1))
        spread_out = dot(jnp.concatenate(rows, axis=0), swap)
        for part in range(2):
            for h in range(pair):
                for u in range(groups):
                    k = (step * pair + h) * groups + u
                    for t in range(tiles):
                        at = (part * pair + h) * span + t * tall
                        p_ref[part, t, pl.ds(k, tall, stride=drift), :] = spread_out[
                            at : at + tall, u * LANE : (u + 1) * LANE
                        ]
        return carry

    transform(0, 0)

    def gather(i):
        c = slab ^ (slabs - 1 - i)
        rec = load(c)
        spot, cell = cells(rec)
        z_ref[0] = place(spline_weights(rec[3:4]), cell, z_ref.shape[1])
        z_ref[1] = place(spline_slopes(rec[3:4]), cell, z_ref.shape[1])
        y_low = [y_ref[c, part] for part in range(2)]
        slopes = [[], []]
        hot_ref[0] = hot_rows(spot)
        for z in range(spots):
            here = tile_of(hot_ref[0, z : z + 1])
            for part in range(2):
                slopes[part] += [y_low[part][j : j + 16] * here for j in range(0, ky, 16)]
        slope_spots = jnp.concatenate(slopes[0] + slopes[1], axis=0)
        following = (c + 1) % slabs
        planes_of = []
        for part in range(2):

            def plane(t, slab_of, z):
                return p_ref[part, t, pl.ds(pl.multiple_of((slab_of * fine + z) * drift, 8), kx), :]

            mains = [jnp.concatenate([plane(t, c, z) for t in range(tiles)], axis=1) for z in range(fine)]
            extras = [
                jnp.concatenate([mains[z][:, ky:], plane(0, following, z)[:, :ky]], axis=1)
                for z in range(REACH - 1)
            ]
            planes_of.append(near(jnp.concatenate(mains + extras, axis=0)))
        lefts = (
            jnp.concatenate([planes_of[0], planes_of[1]], axis=1),
            jnp.concatenate([planes_of[1], -planes_of[0]], axis=1),
        )
        totals = [jnp.zeros((kx, width), f32)] * 4
        for part in range(2):
            level = dot(lefts[part], spots_ref[c])
            slope = dot(lefts[part], slope_spots)
            q = qd = qz = None
            for z in range(reach):
                w = z_ref[0, z : z + 1]
                d = z_ref[1, z : z + 1]
                here = level[z * kx : (z + 1) * kx]
                there = slope[z * kx : (z + 1) * kx]
                q = here * w if q is None else q + here * w
                qz = here * d if qz is None else qz + here * d
                qd = there * w if qd is None else qd + there * w
            x, dx = x_ref[c, part], x_ref[c, 2 + part]
            totals = [totals[0] + x * q, totals[1] + dx * q, totals[2] + x * qd, totals[3] + x * qz]
        terms = jnp.concatenate([jnp.sum(t, axis=0, keepdims=True) for t in totals], axis=0)
        for j in range(grp):
            terms_ref[c * grp + j] = terms[:, j * atoms : (j + 1) * atoms]

    def deliver(i):
        c = slab ^ (slabs - 1 - i)
        for j in range(grp):
            at = c * grp + j

            @pl.when(at == me)
            def _():
                pltpu.make_async_copy(terms_ref.at[at], held_ref.at[me], got_terms).start()

            @pl.when(at != me)
            def _():
                pltpu.make_async_remote_copy(
                    src_ref=terms_ref.at[at],
                    dst_ref=held_ref.at[me],
                    send_sem=sent_terms,
                    recv_sem=got_terms,
                    device_id=(j, c),
                    device_id_type=pl.DeviceIdType.MESH,
                ).start()

    def gather_two(j, carry):
        gather(2 * j)
        gather(2 * j + 1)
        deliver(2 * j)
        deliver(2 * j + 1)
        return carry

    lax.fori_loop(0, slabs // 2, gather_two, 0)
    all_sent(held_ref, total_slots, got_terms)
    all_sent(held_ref, total_slots - 1, sent_terms)
    all_sent(atoms_ref, total_slots - 1, sent)
    factors = jnp.concatenate([live, loaded, loaded, loaded], axis=0)
    out_ref[...] = jnp.sum(held_ref[...], axis=0) * factors


def ring_of(slabs, groups):
    total = slabs * groups
    me = lax.axis_index("pme") * groups + lax.axis_index("grp")

    def peer(i):
        at = me ^ i if total & (total - 1) == 0 else (me + i) % total
        return at, {
            "device_id": (at % groups, at // groups),
            "device_id_type": pl.DeviceIdType.MESH,
        }

    return me, total, peer


def meet(total, peer):
    barrier = pltpu.get_barrier_semaphore()

    def signal(i, carry):
        pl.semaphore_signal(barrier, inc=1, **peer(i)[1])
        return carry

    lax.fori_loop(1, total, signal, 0)
    return lambda: pl.semaphore_wait(barrier, total - 1)


def all_sent(ref, total, sem):
    part = ref.at[pl.ds(0, total)]
    pltpu.make_async_copy(part, part, sem).wait()


def live_of(counts_ref, shape):
    return jnp.where(lax.broadcasted_iota(jnp.int32, shape, 1) < counts_ref[0], 1.0, 0.0)


def body(slabs, groups, charge, base, frac, counts, green):
    atoms = charge.shape[0]
    kx, ky, nz = green.shape
    ny = ky * slabs
    planes = nz // slabs
    if fits(kx, ky, planes, slabs, atoms, FINE):
        return slab_body(slabs, groups, FINE, charge, base, frac, counts, green)
    slots = slabs * groups
    per = math.gcd(groups, 4)
    chunks = slots // per
    smem = pl.BlockSpec(memory_space=pltpu.SMEM)
    vmem = pl.BlockSpec(memory_space=VMEM)
    free = pl.BlockSpec(memory_space=pl.ANY)
    dma = pltpu.SemaphoreType.DMA
    index = np.arange(nz // 2)
    waves = np.stack([2 * index, 2 * index + 1])
    angle = (index[None, :, None] * waves[:, None, :] % nz) * (2.0 * math.pi / nz)
    cosine = np.cos(angle).astype(ml_dtypes.bfloat16)
    sine = np.sin(angle).astype(ml_dtypes.bfloat16)
    count = kx * ky
    width = per * atoms
    low_type = jnp.bfloat16
    wide = ky % 16 == 0
    return pl.pallas_call(
        functools.partial(mesh_kernel, (kx, ky, nz, ny, planes, groups, per, chunks, slabs)),
        out_shape=jax.ShapeDtypeStruct((4, atoms), jnp.float32),
        in_specs=[smem] + [vmem] * 3 + [free] * 3,
        out_specs=vmem,
        scratch_shapes=[
            VMEM((8, atoms), jnp.float32),
            VMEM((slots, 8, atoms), jnp.float32),
            VMEM((slots, 4, atoms), jnp.float32),
            VMEM((slots, 4, atoms), jnp.float32),
            VMEM((count, nz), jnp.float32),
            VMEM((2, nz // 2, nz // 2), low_type),
            VMEM((2, nz // 2, nz // 2), low_type),
            VMEM((chunks, 2 * count, width), low_type),
            VMEM((2 * count, width), low_type),
            VMEM((nz // LANE, 2 * count, LANE), jnp.float32),
            VMEM((2 * count, width), low_type),
            VMEM((nz + 16, 2 * count), low_type),
            VMEM((chunks, 4, kx, width) if wide else (1, 4, 8, LANE), jnp.float32),
            VMEM((chunks, 4, ky, width) if wide else (1, 4, 8, LANE), low_type),
            dma,
            dma((slabs,)),
            dma,
            dma,
            dma((3,)),
        ],
        compiler_params=pltpu.CompilerParams(
            collective_id=1, has_side_effects=True, vmem_limit_bytes=60 * 1024 * 1024
        ),
    )(counts, charge.reshape(1, atoms), frac, base, green.reshape(count, nz), cosine, sine)

def turns_of(nz, planes, fine, groups, tiles, fewer):
    quarter = nz // 4
    g, t, p, z = np.meshgrid(
        np.arange(groups), np.arange(tiles), np.arange(fewer), np.arange(fine), indexing="ij"
    )
    place_of = (p * planes + (t * groups + g) * fine + z).reshape(-1)
    ahead = []
    for r in range(4):
        wave = 4 * np.arange(quarter) + r
        angle = (wave[:, None] * place_of[None, :] % nz) * (2.0 * math.pi / nz)
        cosine, sine = np.cos(angle), np.sin(angle)
        ahead.append(np.block([[cosine, sine], [-sine, cosine]]))
    ahead = np.stack(ahead)
    return ahead.astype(ml_dtypes.bfloat16), ahead.transpose(0, 2, 1).astype(ml_dtypes.bfloat16)


def fits(kx, ky, planes, slabs, atoms, fine):
    if ky % 16 or LANE % ky or kx % 16 or slabs % 4 or planes % fine or atoms % LANE:
        return False
    if slabs & (slabs - 1) or kx > 64 or ky > 64:
        return False
    groups = LANE // ky
    return (
        (planes // fine) % groups == 0
        and kx % groups == 0
        and (slabs // 4 * fine) % 16 == 0
        and fine % 8 == 0
        and fine + REACH - 1 <= 24
    )


def slab_body(slabs, groups, fine, charge, base, frac, counts, green):
    atoms = charge.shape[0]
    kx, ky, nz = green.shape
    ny = ky * slabs
    planes = nz // slabs
    slots = slabs * groups
    width = groups * atoms
    count = kx * ky
    spots = planes // fine
    sets = LANE // ky
    tiles = spots // sets
    ahead, back = turns_of(nz, planes, fine, sets, tiles, slabs // 4)
    vmem = pl.BlockSpec(memory_space=VMEM)
    free = pl.BlockSpec(memory_space=pl.ANY)
    dma = pltpu.SemaphoreType.DMA
    low_type = jnp.bfloat16
    f32 = jnp.float32
    tall = slabs * fine
    reach = fine + REACH - 1
    return pl.pallas_call(
        functools.partial(slab_kernel, (kx, ky, nz, ny, planes, groups, slabs, fine)),
        out_shape=jax.ShapeDtypeStruct((4, atoms), f32),
        in_specs=[free] * 7,
        out_specs=vmem,
        scratch_shapes=[
            pltpu.SMEM((1,), jnp.int32),
            VMEM((1, atoms), f32),
            VMEM((3, atoms), f32),
            VMEM((3, atoms), jnp.int32),
            VMEM((8, atoms), f32),
            VMEM((slots, 8, atoms), f32),
            VMEM((slots, 4, atoms), f32),
            VMEM((slots, 4, atoms), f32),
            VMEM((count, nz), f32),
            VMEM((nz, count), f32),
            VMEM(ahead.shape, low_type),
            VMEM(back.shape, low_type),
            VMEM((2, tiles, kx * (tall + PAD), LANE), f32),
            VMEM((2, tiles, tall * (kx + PAD), LANE), f32),
            VMEM((slabs, 4, kx, width), f32),
            VMEM((slabs, 2, ky, width), low_type),
            VMEM((slabs, 2 * spots * ky, width), low_type),
            VMEM((2, 24, width), f32),
            VMEM((2, spots, width), f32),
            VMEM((2 * reach * kx, width), low_type),
            VMEM((2 * reach * kx, width), low_type),
            VMEM((2 * spots * ky, width), low_type),
            VMEM((2 * spots * ky, width), low_type),
            dma,
            dma((slabs,)),
            dma,
            dma,
            dma((7,)),
        ],
        compiler_params=pltpu.CompilerParams(
            collective_id=2, has_side_effects=True, vmem_limit_bytes=60 * 1024 * 1024
        ),
    )(counts, charge.reshape(1, atoms), frac, base, green.reshape(count, nz), ahead, back)


def solution(mesh):
    placed = (
        P(("grp", "pme")),
        P(None, ("grp", "pme")),
        P(None, ("grp", "pme")),
        P(("grp", "pme")),
        P("grp", "pme", None),
    )
    return jax.shard_map(
        functools.partial(body, mesh.shape["pme"], mesh.shape["grp"]),
        mesh=mesh,
        in_specs=placed,
        out_specs=P(None, ("grp", "pme")),
        check_vma=False,
    )
```

```python
import functools
import math

import jax
import jax.numpy as jnp
import ml_dtypes
import numpy as np
from jax import lax
from jax.experimental import pallas as pl
from jax.experimental.pallas import tpu as pltpu
from jax.sharding import PartitionSpec as P

NX = 256
LANE = 128
REACH = 4
FINE = 16
PAD = 8
VMEM = pltpu.VMEM


def spline_weights(u):
    v = 1.0 - u
    u2 = u * u
    u3 = u2 * u
    return (
        v * v * v / 6.0,
        (3.0 * u3 - 6.0 * u2 + 4.0) / 6.0,
        (-3.0 * u3 + 3.0 * u2 + 3.0 * u + 1.0) / 6.0,
        u3 / 6.0,
    )


def spline_slopes(u):
    v = 1.0 - u
    u2 = u * u
    return (
        -v * v / 2.0,
        (3.0 * u2 - 4.0 * u) / 2.0,
        (-3.0 * u2 + 2.0 * u + 1.0) / 2.0,
        u2 / 2.0,
    )


def turn_parts(turns):
    x = (turns - jnp.floor(turns + 0.5)) * math.pi
    y = x * x
    s = 1.0 / 362880.0 - y * (1.0 / 39916800.0)
    s = -1.0 / 5040.0 + y * s
    s = 1.0 / 120.0 + y * s
    s = -1.0 / 6.0 + y * s
    s = x + x * (y * s)
    c = -1.0 / 3628800.0 + y * (1.0 / 479001600.0)
    c = 1.0 / 40320.0 + y * c
    c = -1.0 / 720.0 + y * c
    c = 1.0 / 24.0 + y * c
    c = -0.5 + y * c
    c = 1.0 + y * c
    return (1.0 - 2.0 * s * s, 2.0 * s * c)


def waves_of(weight_sets, cell, waves, steps):
    copies = cell.shape[1] // waves.shape[1]

    def widen(v):
        return jnp.concatenate([v] * copies, axis=1)

    cb, sb = turn_parts(widen(waves) * cell)
    cosines = [widen(c) for c, _ in steps]
    sines = [widen(s) for _, s in steps]
    out = []
    for w in weight_sets:
        gr = w[0] + sum(w[j + 1] * cosines[j] for j in range(REACH - 1))
        gi = sum(w[j + 1] * sines[j] for j in range(REACH - 1))
        out.append((cb * gr - sb * gi, -(cb * gi + sb * gr)))
    return out


def low(values):
    return values.astype(jnp.bfloat16).astype(jnp.float32)


def place(weights, cell, rows):
    z = lax.broadcasted_iota(jnp.int32, (rows, cell.shape[1]), 0) - cell
    total = jnp.where(z == 0, weights[0], 0.0)
    for j in range(1, REACH):
        total = jnp.where(z == j, weights[j], total)
    return total


def mesh_kernel(
    dims, counts_ref, charge_ref, frac_ref, base_ref, green_in, cos_in, sin_in, out_ref,
    mine_ref, atoms_ref, terms_ref, held_ref, green_ref, cos_ref, sin_ref,
    a_ref, b_ref, s_ref, h_ref, p_ref, x_ref, y_ref, sent, got, sent_terms, got_terms, staged
):
    kx, ky, nz, ny, planes, grp, per, chunks, slabs = dims
    group, slab = lax.axis_index("grp"), lax.axis_index("pme")
    me, total_slots, peer = ring_of(slabs, grp)
    wait = meet(total_slots, peer)
    stages = [
        pltpu.make_async_copy(source, target, staged.at[i])
        for i, (source, target) in enumerate(
            [(green_in, green_ref), (cos_in, cos_ref), (sin_in, sin_ref)]
        )
    ]
    for stage in stages:
        stage.start()
    live = live_of(counts_ref, charge_ref.shape)
    loaded = charge_ref[...] * live
    mine_ref[...] = jnp.concatenate(
        [loaded, frac_ref[...], base_ref[...].astype(jnp.float32), live], axis=0
    )
    own = pltpu.make_async_copy(mine_ref, atoms_ref.at[me], got.at[slab])
    own.start()
    count = kx * ky
    width = per * LANE
    tiles = nz // LANE
    fine = min(64, LANE)
    rows = fine + 16
    wide = ky % 16 == 0

    if wide:
        xk = lax.broadcasted_iota(jnp.int32, (kx, LANE), 0)
        yk = lax.broadcasted_iota(jnp.int32, (ky, LANE), 0)
    else:
        index = lax.broadcasted_iota(jnp.int32, (count, LANE), 0)
        xk, yk = index // ky, index % ky
    xk = (xk + group * kx).astype(jnp.float32) * (1.0 / NX)
    yk = (yk + slab * ky).astype(jnp.float32) * (1.0 / ny)
    x_steps = [turn_parts(xk * j) for j in range(1, REACH)]
    y_steps = [turn_parts(yk * j) for j in range(1, REACH)]

    s_ref[...] = jnp.zeros_like(s_ref)
    dot = functools.partial(jnp.dot, preferred_element_type=jnp.float32)
    half = nz // 2
    scale = 1.0 / (ny * nz)
    for stage in stages:
        stage.wait()
    lane_in = lax.broadcasted_iota(jnp.int32, (nz, nz), 0)
    lane_out = lax.broadcasted_iota(jnp.int32, (nz, nz), 1)
    wanted = jnp.where(lane_out < half, 2 * lane_out, 2 * (lane_out - half) + 1)
    order = jnp.where(lane_in == wanted, 1.0, 0.0).astype(jnp.bfloat16)
    block = min(256, count)
    for k in range(0, count, block):
        whole = green_ref[k : k + block] * scale
        high = whole.astype(jnp.bfloat16)
        rest = (whole - high.astype(jnp.float32)).astype(jnp.bfloat16)
        green_ref[k : k + block] = dot(high, order) + dot(rest, order)
    wait()

    def send(i, carry):
        pltpu.make_async_remote_copy(
            src_ref=mine_ref,
            dst_ref=atoms_ref.at[me],
            send_sem=sent,
            recv_sem=got.at[slab],
            **peer(i)[1],
        ).start()
        return carry

    lax.fori_loop(1, total_slots, send, 0)
    share = grp // per

    def turn_to(i, ahead):
        return (slab + ahead + i // share) % slabs * share + i % share

    def load(c):
        return jnp.concatenate([atoms_ref[c * per + i] for i in range(per)], axis=1)

    def tables(rec):
        fx, fy = rec[1:2], rec[2:3]
        wx = [spline_weights(fx), spline_slopes(fx)]
        wy = [[low(w) for w in spline_weights(fy)], [low(w) for w in spline_slopes(fy)]]
        return waves_of(wx, rec[4:5], xk, x_steps), waves_of(wy, rec[5:6], yk, y_steps)

    def keep(c, rec):
        for kind, (x, y) in enumerate(zip(*tables(rec))):
            for part in range(2):
                x_ref[c, 2 * kind + part] = x[part]
                y_ref[c, 2 * kind + part] = y[part].astype(jnp.bfloat16)

    def row_of(c, kind, i):
        return [
            jnp.broadcast_to(x_ref[c, 2 * kind + part, i : i + 1], (16, width)).astype(jnp.bfloat16)
            for part in range(2)
        ]

    def product(ref, lead, c, x_kind, y_kind, made):
        if not wide:
            (xr, xi), (yr, yi) = made[0][x_kind], made[1][y_kind]
            ref[lead + (slice(0, count),)] = (xr * yr - xi * yi).astype(jnp.bfloat16)
            ref[lead + (slice(count, 2 * count),)] = (xr * yi + xi * yr).astype(jnp.bfloat16)
            return
        for i in range(kx):
            row = row_of(c, x_kind, i)
            for j in range(0, ky, 16):
                yr = y_ref[c, 2 * y_kind, j : j + 16]
                yi = y_ref[c, 2 * y_kind + 1, j : j + 16]
                at = i * ky + j
                ref[lead + (slice(at, at + 16),)] = row[0] * yr - row[1] * yi
                ref[lead + (slice(count + at, count + at + 16),)] = row[0] * yi + row[1] * yr

    def arrive(i):
        c = turn_to(i, 0)

        @pl.when(i % share == 0)
        def _():
            part = atoms_ref.at[pl.ds(c * per, grp)]
            pltpu.make_async_copy(part, part, got.at[c // share]).wait()

        return c

    def spread(i, carry):
        c = arrive(i)
        rec = load(c)
        start = (c * per) // grp * planes
        tile = start // LANE
        cell = rec[6:7].astype(jnp.int32) + (start - tile * LANE)
        wz = [rec[0:1] * w for w in spline_weights(rec[3:4])]
        table = place(wz, cell, LANE + 16).astype(jnp.bfloat16)
        rest = jnp.zeros((LANE - 16, width), jnp.bfloat16)
        table = jnp.concatenate([table, rest], axis=0)
        following = lax.rem(tile + 1, tiles)

        def add(at, size, block):
            part = lax.dot_general(
                block, table, (((1,), (1,)), ((), ())), preferred_element_type=jnp.float32
            )
            s_ref[tile, at : at + size] += part[:, :LANE]
            s_ref[following, at : at + size] += part[:, LANE:]

        if not wide:
            product(a_ref, (c,), c, 0, 0, tables(rec))
            add(0, 2 * count, a_ref[c])
            return carry
        keep(c, rec)
        some = max(1, 256 // ky)
        for i0 in range(0, kx, some):
            blocks = ([], [])
            for k in range(i0, min(i0 + some, kx)):
                row = row_of(c, 0, k)
                for j in range(0, ky, 16):
                    yr, yi = y_ref[c, 0, j : j + 16], y_ref[c, 1, j : j + 16]
                    blocks[0].append(row[0] * yr - row[1] * yi)
                    blocks[1].append(row[0] * yi + row[1] * yr)
            for part in range(2):
                block = jnp.concatenate(blocks[part], axis=0)
                at, size = part * count + i0 * ky, block.shape[0]
                a_ref[c, at : at + size] = block
                add(at, size, block)
        return carry

    lax.fori_loop(0, chunks, spread, 0)

    def dot_t(a, b):
        return lax.dot_general(a, b, (((1,), (1,)), ((), ())), preferred_element_type=jnp.float32)

    def near(values):
        return values.astype(jnp.bfloat16)

    middle = tiles // 2
    for k in range(0, count, block):
        back = []
        parts = []
        for at in (k, count + k):
            first = jnp.concatenate([s_ref[t, at : at + block] for t in range(middle)], axis=1)
            last = jnp.concatenate([s_ref[t, at : at + block] for t in range(middle, tiles)], axis=1)
            parts.append((near(first + last), near(first - last)))
        for odd in range(2):
            cosine, sine = cos_ref[odd], sin_ref[odd]
            sr, si = parts[0][odd], parts[1][odd]
            factor = green_ref[k : k + block, odd * half : (odd + 1) * half]
            hr = near((dot(sr, cosine) + dot(si, sine)) * factor)
            hi = near((dot(si, cosine) - dot(sr, sine)) * factor)
            back.append((dot_t(cosine, hr) - dot_t(sine, hi), dot_t(cosine, hi) + dot_t(sine, hr)))
        for part, at in enumerate((k, count + k)):
            even, odd = back[0][part], back[1][part]
            lower = near(even + odd)
            p_ref[0:half, at : at + block] = lower
            p_ref[half:nz, at : at + block] = near(even - odd)
            p_ref[nz : nz + 16, at : at + block] = lower[0:16]

    def gather(i, carry):
        c = turn_to(i, 1)
        rec = load(c)
        made = None if wide else tables(rec)
        product(b_ref, (), c, 1, 0, made)
        product(h_ref, (), c, 0, 1, made)
        start = (c * per) // grp * planes
        base = start // fine * fine
        cell = rec[6:7].astype(jnp.int32) + (start - base)
        window = p_ref[pl.ds(pl.multiple_of(base, 16), rows), :]
        level = dot(window, a_ref[c])
        along_x = dot(window, b_ref[...])
        along_y = dot(window, h_ref[...])
        wz = place(spline_weights(rec[3:4]), cell, rows)
        dz = place(spline_slopes(rec[3:4]), cell, rows)

        def total(values):
            return jnp.sum(values, axis=0, keepdims=True)

        terms = jnp.concatenate(
            [total(wz * level), total(wz * along_x), total(wz * along_y), total(dz * level)], axis=0
        )
        for j in range(per):
            at = c * per + j
            terms_ref[at] = terms[:, j * LANE : (j + 1) * LANE]

            @pl.when(at == me)
            def _():
                pltpu.make_async_copy(terms_ref.at[at], held_ref.at[me], got_terms).start()

            @pl.when(at != me)
            def _():
                pltpu.make_async_remote_copy(
                    src_ref=terms_ref.at[at],
                    dst_ref=held_ref.at[me],
                    send_sem=sent_terms,
                    recv_sem=got_terms,
                    device_id=(at % grp, at // grp),
                    device_id_type=pl.DeviceIdType.MESH,
                ).start()

        return carry

    lax.fori_loop(0, chunks, gather, 0)
    all_sent(held_ref, total_slots, got_terms)
    all_sent(held_ref, total_slots - 1, sent_terms)
    all_sent(atoms_ref, total_slots - 1, sent)
    factors = jnp.concatenate([live, loaded, loaded, loaded], axis=0)
    out_ref[...] = jnp.sum(held_ref[...], axis=0) * factors

def digits(value, radix):
    return value // radix, value % radix


def waves_by_parts(weight_sets, cell, first, unit, steps):
    width = cell.shape[1]
    count = steps[0][0].shape[0]
    copies = width // LANE
    low_rows = lax.broadcasted_iota(jnp.int32, (8, width), 0)
    fine_c, fine_s = turn_parts(low_rows.astype(jnp.float32) * unit * cell)
    coarse_rows = (first + 8 * low_rows).astype(jnp.float32) * unit
    coarse_c, coarse_s = turn_parts(coarse_rows * cell)

    def widen(v):
        return jnp.concatenate([v] * copies, axis=1)

    cosines = [widen(c) for c, _ in steps]
    sines = [widen(s) for _, s in steps]
    turned = []
    for i in range(count // 8):
        c, s = coarse_c[i : i + 1], coarse_s[i : i + 1]
        turned.append((c * fine_c - s * fine_s, s * fine_c + c * fine_s))
    cb = jnp.concatenate([c for c, _ in turned], axis=0)
    sb = jnp.concatenate([s for _, s in turned], axis=0)
    out = []
    for w in weight_sets:
        gr = w[0] + sum(w[j + 1] * cosines[j] for j in range(REACH - 1))
        gi = sum(w[j + 1] * sines[j] for j in range(REACH - 1))
        out.append((cb * gr - sb * gi, -(cb * gi + sb * gr)))
    return out


def slab_kernel(
    dims, counts_in, charge_in, frac_in, base_in, green_in, ahead_in, back_in, out_ref,
    counts_ref, charge_ref, frac_ref, base_ref,
    mine_ref, atoms_ref, terms_ref, held_ref, green_ref, turned_ref, ahead_ref, back_ref,
    s_ref, p_ref, x_ref, y_ref, spots_ref, z_ref, hot_ref,
    left_0, left_1, right_0, right_1, sent, got, sent_terms, got_terms, staged
):
    kx, ky, nz, ny, planes, grp, slabs, fine = dims
    group, slab = lax.axis_index("grp"), lax.axis_index("pme")
    me, total_slots, peer = ring_of(slabs, grp)
    wait = meet(total_slots, peer)
    stages = [
        pltpu.make_async_copy(source, target, staged.at[i])
        for i, (source, target) in enumerate(
            [
                (counts_in, counts_ref),
                (charge_in, charge_ref),
                (frac_in, frac_ref),
                (base_in, base_ref),
                (green_in, green_ref),
                (ahead_in, ahead_ref),
                (back_in, back_ref),
            ]
        )
    ]
    for stage in stages:
        stage.start()
    for stage in stages[:4]:
        stage.wait()
    live = live_of(counts_ref, charge_ref.shape)
    loaded = charge_ref[...] * live
    mine_ref[...] = jnp.concatenate(
        [loaded, frac_ref[...], base_ref[...].astype(jnp.float32), live], axis=0
    )
    own = pltpu.make_async_copy(mine_ref, atoms_ref.at[me], got.at[slab])
    own.start()

    atoms = charge_ref.shape[1]
    width = grp * atoms
    groups = LANE // ky
    spots = planes // fine
    tiles = spots // groups
    lanes = spots * ky
    reach = fine + REACH - 1
    tall = slabs * fine
    pitch = tall + PAD
    drift = kx + PAD
    quarter = nz // 4
    low_type = jnp.bfloat16
    f32 = jnp.float32
    left_refs, right_refs = (left_0, left_1), (right_0, right_1)
    dot = functools.partial(jnp.dot, preferred_element_type=f32)

    def dot_t(a, b):
        return lax.dot_general(a, b, (((1,), (1,)), ((), ())), preferred_element_type=f32)

    xk = (lax.broadcasted_iota(jnp.int32, (kx, LANE), 0) + group * kx).astype(f32) * (1.0 / NX)
    yk = (lax.broadcasted_iota(jnp.int32, (ky, LANE), 0) + slab * ky).astype(f32) * (1.0 / ny)
    x_steps = [turn_parts(xk * j) for j in range(1, REACH)]
    y_steps = [turn_parts(yk * j) for j in range(1, REACH)]

    for part in range(2):
        for t in range(tiles):
            for z in range(REACH - 1):
                for p in range(slabs):
                    s_ref[part, t, pl.ds(p * fine + z, kx, stride=pitch), :] = jnp.zeros((kx, LANE), f32)
    for stage in stages[4:]:
        stage.wait()
    row = lax.broadcasted_iota(jnp.int32, (nz, nz), 0)
    column = lax.broadcasted_iota(jnp.int32, (nz, nz), 1)
    wanted = 4 * (row % quarter) + row // quarter
    order = jnp.where(column == wanted, 1.0, 0.0).astype(low_type)
    scale = 1.0 / (ny * nz)
    block = 2 * LANE
    for k in range(0, kx * ky, block):
        whole = green_ref[k : k + block] * scale
        high = whole.astype(low_type)
        rest = (whole - high.astype(f32)).astype(low_type)
        turned_ref[:, k : k + block] = dot_t(order, high) + dot_t(order, rest)
    wait()

    def send(i, carry):
        pltpu.make_async_remote_copy(
            src_ref=mine_ref,
            dst_ref=atoms_ref.at[me],
            send_sem=sent,
            recv_sem=got.at[slab],
            **peer(i)[1],
        ).start()
        return carry

    lax.fori_loop(1, total_slots, send, 0)

    def load(c):
        return jnp.concatenate([atoms_ref[c * grp + i] for i in range(grp)], axis=1)

    def cells(rec):
        cell = rec[6:7].astype(jnp.int32)
        return digits(cell, fine)

    def tile_of(row):
        return jnp.broadcast_to(row, (16, width)).astype(low_type)

    def hot_rows(spot):
        return jnp.where(lax.broadcasted_iota(jnp.int32, (spots, width), 0) == spot, 1.0, 0.0)

    def arrive(i):
        c = slab ^ i
        part = atoms_ref.at[pl.ds(c * grp, grp)]
        pltpu.make_async_copy(part, part, got.at[c]).wait()

    def build(i, side_of):
        c = slab ^ i
        rec = load(c)
        fx, fy, fz = rec[1:2], rec[2:3], rec[3:4]
        wx = [spline_weights(fx), spline_slopes(fx)]
        wy = [[low(w) for w in spline_weights(fy)], [low(w) for w in spline_slopes(fy)]]
        xs = waves_by_parts(wx, rec[4:5], group * kx, 1.0 / NX, x_steps)
        ys = waves_by_parts(wy, rec[5:6], slab * ky, 1.0 / ny, y_steps)
        for kind in range(2):
            for part in range(2):
                x_ref[c, 2 * kind + part] = xs[kind][part]
        for part in range(2):
            y_ref[c, part] = ys[1][part].astype(low_type)
        spot, cell = cells(rec)
        y_low = [ys[0][part].astype(low_type) for part in range(2)]
        hot_ref[side_of] = hot_rows(spot)
        for z in range(spots):
            here = tile_of(hot_ref[side_of, z : z + 1])
            for part in range(2):
                for j in range(0, ky, 16):
                    at = part * lanes + z * ky + j
                    made = y_low[part][j : j + 16] * here
                    spots_ref[c, at : at + 16] = made
                    right_refs[side_of][at : at + 16] = made
        z_ref[side_of] = place(spline_weights(fz), cell, z_ref.shape[1])
        x_low = [(xs[0][part] * rec[0:1]).astype(low_type) for part in range(2)]
        at = 0
        for z in range(reach):
            weight = tile_of(z_ref[side_of, z : z + 1])
            for part in range(2):
                for j in range(0, kx, 16):
                    left_refs[side_of][at : at + 16] = x_low[part][j : j + 16] * weight
                    at += 16

    def mix(i, side_of):
        c = slab ^ i
        made = dot_t(left_refs[side_of][...], right_refs[side_of][...])

        def mesh_rows(z):
            at = 2 * z * kx
            real, imag = made[at : at + kx], made[at + kx : at + 2 * kx]
            return (
                real[:, :lanes] - imag[:, lanes:],
                real[:, lanes:] + imag[:, :lanes],
            )

        following = (c + 1) % slabs
        first = lax.broadcasted_iota(jnp.int32, (kx, lanes), 1) < ky

        def rows_at(slab_of, z):
            return pl.ds(slab_of * fine + z, kx, stride=pitch)

        held = {}
        for z in range(REACH - 1):
            for part in range(2):
                for t in range(tiles):
                    held[z, part, t] = s_ref[part, t, rows_at(c, z), :]
                held[z, part] = s_ref[part, 0, rows_at(following, z), :]
        for z in range(fine):
            values = mesh_rows(z)
            past = mesh_rows(z + fine) if z + fine < reach else None
            for part in range(2):
                value = values[part]
                if past is not None:
                    moved = jnp.concatenate(
                        [past[part][:, lanes - ky :], past[part][:, : lanes - ky]], axis=1
                    )
                    value = value + jnp.where(first, 0.0, moved)
                    s_ref[part, 0, rows_at(following, z), :] = (
                        held[z, part] + jnp.where(first, moved, 0.0)[:, :LANE]
                    )
                for t in range(tiles):
                    out = value[:, t * LANE : (t + 1) * LANE]
                    if past is not None:
                        out = out + held[z, part, t]
                    s_ref[part, t, rows_at(c, z), :] = out

    def two(j, carry):
        arrive(2 * j + 1)
        arrive(2 * j + 2)
        mix(2 * j, 0)
        build(2 * j + 1, 1)
        mix(2 * j + 1, 1)
        build(2 * j + 2, 0)
        return carry

    arrive(0)
    build(0, 0)
    lax.fori_loop(0, slabs // 2 - 1, two, 0)
    arrive(slabs - 1)
    mix(slabs - 2, 0)
    build(slabs - 1, 1)
    mix(slabs - 1, 1)

    side = groups * LANE
    row = lax.broadcasted_iota(jnp.int32, (side, side), 0)
    column = lax.broadcasted_iota(jnp.int32, (side, side), 1)
    wanted = (row % LANE) // ky * LANE + row // LANE * ky + row % ky
    swap = jnp.where(column == wanted, 1.0, 0.0).astype(low_type)
    fewer = slabs // 4
    piece = fewer * fine
    pair = kx // groups

    def near(values):
        return values.astype(low_type)

    def transform(step, carry):
        lefts = []
        for part in range(2):
            for g in range(pair):
                k0 = (step * pair + g) * groups
                for t in range(tiles):
                    lefts.append(
                        jnp.concatenate(
                            [
                                near(s_ref[part, t, pl.ds(pl.multiple_of((k0 + u) * pitch, 8), tall), :])
                                for u in range(groups)
                            ],
                            axis=1,
                        )
                    )
        swapped = dot(jnp.concatenate(lefts, axis=0), swap)
        span = tiles * tall
        picked = []
        for part in range(2):
            halves = [swapped[(part * pair + g) * span : (part * pair + g + 1) * span] for g in range(pair)]
            quarters = []
            for m in range(4):
                blocks = []
                for g in range(groups):
                    for t in range(tiles):
                        at = t * tall + m * piece
                        blocks.append(
                            jnp.concatenate(
                                [half[at : at + piece, g * LANE : (g + 1) * LANE] for half in halves], axis=1
                            )
                        )
                quarters.append(jnp.concatenate(blocks, axis=0))
            picked.append(quarters)
        re, im = picked
        ar, ai, br, bi = re[0] + re[2], im[0] + im[2], re[0] - re[2], im[0] - im[2]
        cr, ci, dr, di = re[1] + re[3], im[1] + im[3], re[1] - re[3], im[1] - im[3]
        mixed = [(ar + cr, ai + ci), (br + di, bi - dr), (ar - cr, ai - ci), (br - di, bi + dr)]
        back = []
        for r in range(4):
            stacked = jnp.concatenate([near(mixed[r][0]), near(mixed[r][1])], axis=0)
            waves = dot(ahead_ref[r], stacked)
            at = pl.ds(pl.multiple_of(step * pair * LANE, LANE), pair * LANE)
            factor = turned_ref[r * quarter : (r + 1) * quarter, at]
            scaled = jnp.concatenate([near(waves[:quarter] * factor), near(waves[quarter:] * factor)], axis=0)
            mesh = dot(back_ref[r], scaled)
            back.append((mesh[:quarter], mesh[quarter:]))
        er, ei = back[0][0] + back[2][0], back[0][1] + back[2][1]
        fr, fi = back[0][0] - back[2][0], back[0][1] - back[2][1]
        ur, ui = back[1][0] + back[3][0], back[1][1] + back[3][1]
        vr, vi = back[1][0] - back[3][0], back[1][1] - back[3][1]
        quarters = [
            (near(er + ur), near(ei + ui)),
            (near(fr - vi), near(fi + vr)),
            (near(er - ur), near(ei - ui)),
            (near(fr + vi), near(fi - vr)),
        ]
        rows = []
        for part in range(2):
            for h in range(pair):
                columns = []
                for g in range(groups):
                    blocks = []
                    for t in range(tiles):
                        for m in range(4):
                            at = (g * tiles + t) * piece
                            blocks.append(quarters[m][part][at : at + piece, h * LANE : (h + 1) * LANE])
                    columns.append(jnp.concatenate(blocks, axis=0))
                rows.append(jnp.concatenate(columns, axis=1))
        spread_out = dot(jnp.concatenate(rows, axis=0), swap)
        for part in range(2):
            for h in range(pair):
                for u in range(groups):
                    k = (step * pair + h) * groups + u
                    for t in range(tiles):
                        at = (part * pair + h) * span + t * tall
                        p_ref[part, t, pl.ds(k, tall, stride=drift), :] = spread_out[
                            at : at + tall, u * LANE : (u + 1) * LANE
                        ]
        return carry

    transform(0, 0)

    def gather(i):
        c = slab ^ (slabs - 1 - i)
        rec = load(c)
        spot, cell = cells(rec)
        z_ref[0] = place(spline_weights(rec[3:4]), cell, z_ref.shape[1])
        z_ref[1] = place(spline_slopes(rec[3:4]), cell, z_ref.shape[1])
        y_low = [y_ref[c, part] for part in range(2)]
        slopes = [[], []]
        hot_ref[0] = hot_rows(spot)
        for z in range(spots):
            here = tile_of(hot_ref[0, z : z + 1])
            for part in range(2):
                slopes[part] += [y_low[part][j : j + 16] * here for j in range(0, ky, 16)]
        slope_spots = jnp.concatenate(slopes[0] + slopes[1], axis=0)
        following = (c + 1) % slabs
        planes_of = []
        for part in range(2):

            def plane(t, slab_of, z):
                return p_ref[part, t, pl.ds(pl.multiple_of((slab_of * fine + z) * drift, 8), kx), :]

            mains = [jnp.concatenate([plane(t, c, z) for t in range(tiles)], axis=1) for z in range(fine)]
            extras = [
                jnp.concatenate([mains[z][:, ky:], plane(0, following, z)[:, :ky]], axis=1)
                for z in range(REACH - 1)
            ]
            planes_of.append(near(jnp.concatenate(mains + extras, axis=0)))
        lefts = jnp.concatenate(
            [
                jnp.concatenate([planes_of[0], planes_of[1]], axis=1),
                jnp.concatenate([planes_of[1], -planes_of[0]], axis=1),
            ],
            axis=0,
        )
        step = 2 * LANE
        kept = [[], [], [], []]
        for n in range(0, width, step):
            level = dot(lefts, spots_ref[c, :, n : n + step])
            slope = dot(lefts, slope_spots[:, n : n + step])
            totals = [jnp.zeros((kx, step), f32)] * 4
            for part in range(2):
                q = qd = qz = None
                for z in range(reach):
                    w = z_ref[0, z : z + 1, n : n + step]
                    d = z_ref[1, z : z + 1, n : n + step]
                    at = (part * reach + z) * kx
                    here = level[at : at + kx]
                    there = slope[at : at + kx]
                    q = here * w if q is None else q + here * w
                    qz = here * d if qz is None else qz + here * d
                    qd = there * w if qd is None else qd + there * w
                x, dx = x_ref[c, part, :, n : n + step], x_ref[c, 2 + part, :, n : n + step]
                totals = [totals[0] + x * q, totals[1] + dx * q, totals[2] + x * qd, totals[3] + x * qz]
            for row, total in zip(kept, totals):
                row.append(jnp.sum(total, axis=0, keepdims=True))
        terms = jnp.concatenate([jnp.concatenate(row, axis=1) for row in kept], axis=0)
        for j in range(grp):
            terms_ref[c * grp + j] = terms[:, j * atoms : (j + 1) * atoms]

    def deliver(i):
        c = slab ^ (slabs - 1 - i)
        for j in range(grp):
            at = c * grp + j

            @pl.when(at == me)
            def _():
                pltpu.make_async_copy(terms_ref.at[at], held_ref.at[me], got_terms).start()

            @pl.when(at != me)
            def _():
                pltpu.make_async_remote_copy(
                    src_ref=terms_ref.at[at],
                    dst_ref=held_ref.at[me],
                    send_sem=sent_terms,
                    recv_sem=got_terms,
                    device_id=(j, c),
                    device_id_type=pl.DeviceIdType.MESH,
                ).start()

    def gather_two(j, carry):
        gather(2 * j)
        gather(2 * j + 1)
        deliver(2 * j)
        deliver(2 * j + 1)
        return carry

    lax.fori_loop(0, slabs // 2, gather_two, 0)
    all_sent(held_ref, total_slots, got_terms)
    all_sent(held_ref, total_slots - 1, sent_terms)
    all_sent(atoms_ref, total_slots - 1, sent)
    factors = jnp.concatenate([live, loaded, loaded, loaded], axis=0)
    out_ref[...] = jnp.sum(held_ref[...], axis=0) * factors


def ring_of(slabs, groups):
    total = slabs * groups
    me = lax.axis_index("pme") * groups + lax.axis_index("grp")

    def peer(i):
        at = me ^ i if total & (total - 1) == 0 else (me + i) % total
        return at, {
            "device_id": (at % groups, at // groups),
            "device_id_type": pl.DeviceIdType.MESH,
        }

    return me, total, peer


def meet(total, peer):
    barrier = pltpu.get_barrier_semaphore()

    def signal(i, carry):
        pl.semaphore_signal(barrier, inc=1, **peer(i)[1])
        return carry

    lax.fori_loop(1, total, signal, 0)
    return lambda: pl.semaphore_wait(barrier, total - 1)


def all_sent(ref, total, sem):
    part = ref.at[pl.ds(0, total)]
    pltpu.make_async_copy(part, part, sem).wait()


def live_of(counts_ref, shape):
    return jnp.where(lax.broadcasted_iota(jnp.int32, shape, 1) < counts_ref[0], 1.0, 0.0)


def body(slabs, groups, charge, base, frac, counts, green):
    atoms = charge.shape[0]
    kx, ky, nz = green.shape
    ny = ky * slabs
    planes = nz // slabs
    if fits(kx, ky, planes, slabs, atoms, FINE):
        return slab_body(slabs, groups, FINE, charge, base, frac, counts, green)
    slots = slabs * groups
    per = math.gcd(groups, 4)
    chunks = slots // per
    smem = pl.BlockSpec(memory_space=pltpu.SMEM)
    vmem = pl.BlockSpec(memory_space=VMEM)
    free = pl.BlockSpec(memory_space=pl.ANY)
    dma = pltpu.SemaphoreType.DMA
    index = np.arange(nz // 2)
    waves = np.stack([2 * index, 2 * index + 1])
    angle = (index[None, :, None] * waves[:, None, :] % nz) * (2.0 * math.pi / nz)
    cosine = np.cos(angle).astype(ml_dtypes.bfloat16)
    sine = np.sin(angle).astype(ml_dtypes.bfloat16)
    count = kx * ky
    width = per * atoms
    low_type = jnp.bfloat16
    wide = ky % 16 == 0
    return pl.pallas_call(
        functools.partial(mesh_kernel, (kx, ky, nz, ny, planes, groups, per, chunks, slabs)),
        out_shape=jax.ShapeDtypeStruct((4, atoms), jnp.float32),
        in_specs=[smem] + [vmem] * 3 + [free] * 3,
        out_specs=vmem,
        scratch_shapes=[
            VMEM((8, atoms), jnp.float32),
            VMEM((slots, 8, atoms), jnp.float32),
            VMEM((slots, 4, atoms), jnp.float32),
            VMEM((slots, 4, atoms), jnp.float32),
            VMEM((count, nz), jnp.float32),
            VMEM((2, nz // 2, nz // 2), low_type),
            VMEM((2, nz // 2, nz // 2), low_type),
            VMEM((chunks, 2 * count, width), low_type),
            VMEM((2 * count, width), low_type),
            VMEM((nz // LANE, 2 * count, LANE), jnp.float32),
            VMEM((2 * count, width), low_type),
            VMEM((nz + 16, 2 * count), low_type),
            VMEM((chunks, 4, kx, width) if wide else (1, 4, 8, LANE), jnp.float32),
            VMEM((chunks, 4, ky, width) if wide else (1, 4, 8, LANE), low_type),
            dma,
            dma((slabs,)),
            dma,
            dma,
            dma((3,)),
        ],
        compiler_params=pltpu.CompilerParams(
            collective_id=1, has_side_effects=True, vmem_limit_bytes=60 * 1024 * 1024
        ),
    )(counts, charge.reshape(1, atoms), frac, base, green.reshape(count, nz), cosine, sine)

def turns_of(nz, planes, fine, groups, tiles, fewer):
    quarter = nz // 4
    g, t, p, z = np.meshgrid(
        np.arange(groups), np.arange(tiles), np.arange(fewer), np.arange(fine), indexing="ij"
    )
    place_of = (p * planes + (t * groups + g) * fine + z).reshape(-1)
    ahead = []
    for r in range(4):
        wave = 4 * np.arange(quarter) + r
        angle = (wave[:, None] * place_of[None, :] % nz) * (2.0 * math.pi / nz)
        cosine, sine = np.cos(angle), np.sin(angle)
        ahead.append(np.block([[cosine, sine], [-sine, cosine]]))
    ahead = np.stack(ahead)
    return ahead.astype(ml_dtypes.bfloat16), ahead.transpose(0, 2, 1).astype(ml_dtypes.bfloat16)


def fits(kx, ky, planes, slabs, atoms, fine):
    if ky % 16 or LANE % ky or kx % 16 or slabs % 4 or planes % fine or atoms % LANE:
        return False
    if slabs & (slabs - 1) or kx > 64 or ky > 64:
        return False
    groups = LANE // ky
    return (
        (planes // fine) % groups == 0
        and kx % groups == 0
        and (slabs // 4 * fine) % 16 == 0
        and fine % 8 == 0
        and fine + REACH - 1 <= 24
    )


def slab_body(slabs, groups, fine, charge, base, frac, counts, green):
    atoms = charge.shape[0]
    kx, ky, nz = green.shape
    ny = ky * slabs
    planes = nz // slabs
    slots = slabs * groups
    width = groups * atoms
    count = kx * ky
    spots = planes // fine
    sets = LANE // ky
    tiles = spots // sets
    ahead, back = turns_of(nz, planes, fine, sets, tiles, slabs // 4)
    vmem = pl.BlockSpec(memory_space=VMEM)
    free = pl.BlockSpec(memory_space=pl.ANY)
    dma = pltpu.SemaphoreType.DMA
    low_type = jnp.bfloat16
    f32 = jnp.float32
    tall = slabs * fine
    reach = fine + REACH - 1
    return pl.pallas_call(
        functools.partial(slab_kernel, (kx, ky, nz, ny, planes, groups, slabs, fine)),
        out_shape=jax.ShapeDtypeStruct((4, atoms), f32),
        in_specs=[free] * 7,
        out_specs=vmem,
        scratch_shapes=[
            pltpu.SMEM((1,), jnp.int32),
            VMEM((1, atoms), f32),
            VMEM((3, atoms), f32),
            VMEM((3, atoms), jnp.int32),
            VMEM((8, atoms), f32),
            VMEM((slots, 8, atoms), f32),
            VMEM((slots, 4, atoms), f32),
            VMEM((slots, 4, atoms), f32),
            VMEM((count, nz), f32),
            VMEM((nz, count), f32),
            VMEM(ahead.shape, low_type),
            VMEM(back.shape, low_type),
            VMEM((2, tiles, kx * (tall + PAD), LANE), f32),
            VMEM((2, tiles, tall * (kx + PAD), LANE), f32),
            VMEM((slabs, 4, kx, width), f32),
            VMEM((slabs, 2, ky, width), low_type),
            VMEM((slabs, 2 * spots * ky, width), low_type),
            VMEM((2, 24, width), f32),
            VMEM((2, spots, width), f32),
            VMEM((2 * reach * kx, width), low_type),
            VMEM((2 * reach * kx, width), low_type),
            VMEM((2 * spots * ky, width), low_type),
            VMEM((2 * spots * ky, width), low_type),
            dma,
            dma((slabs,)),
            dma,
            dma,
            dma((7,)),
        ],
        compiler_params=pltpu.CompilerParams(
            collective_id=2, has_side_effects=True, vmem_limit_bytes=60 * 1024 * 1024
        ),
    )(counts, charge.reshape(1, atoms), frac, base, green.reshape(count, nz), ahead, back)


def solution(mesh):
    placed = (
        P(("grp", "pme")),
        P(None, ("grp", "pme")),
        P(None, ("grp", "pme")),
        P(("grp", "pme")),
        P("grp", "pme", None),
    )
    return jax.shard_map(
        functools.partial(body, mesh.shape["pme"], mesh.shape["grp"]),
        mesh=mesh,
        in_specs=placed,
        out_specs=P(None, ("grp", "pme")),
        check_vma=False,
    )
```
